512 devices in a mesh: dp: 4 (over x), shard: 128 (over z, y, core).
Axes of the slice: x: 4, y: 8, z: 8, core: 2. Of those that a mesh axis runs over, the one named last changes fastest.
Arguments:
- stats_partial: float32 [4, 128, 2, 512, 512], P('dp', None, None, 'shard'), may hold values from -800 to 800, as said below
- gradient: bfloat16 [128, 512, 512], P(None, 'shard'), may hold values from -240 to 240
- owner_of: int32 [128], replicated, may hold values from 0 to 127, as said below
- layer_count: int32 [4], replicated, may hold values from 1 to 64, 128 in all
Outputs:
- preconditioned: bfloat16 [128, 2, 512, 512], P('shard', None, 'dp')
The draws below stay inside these ranges and needn't reach their ends.
Inputs may be any that keep to these rules, and one draw needn't show every extreme that they name: `owner_of`: each owner holds 0 to 2 blocks, and in every draw some owner holds exactly 2. `layer_count`: the counts sum to 128. `stats_partial`: each [512, 512] slice is symmetric positive definite.
All inputs are finite; a program needn't handle non-finite values.
Results may differ from the reference program's by a relative error of at most 0.0062.
The reference program's roundings to bfloat16 on the way (of `middle`) count: a program that leaves them out, or rounds other values in their place, can miss the bound.
Values may be sent and summed in bfloat16 or wider, within the bound.
No kernel may reach another device: no remote copies, remote signals or barrier semaphores. Data moves between devices by JAX's collectives and lax.ppermute only.
A program may use at most 64 MiB of HBM per device.

```python
import math
import jax
import jax.numpy as jnp
import numpy as np
from jax import lax

B = 512
ITERS = 3
OCAP = 2
LAYERS = 4
NG = 128
N_DP = 4
N_SHARD = 128


def shared_signs(key):
    flips = jax.random.bernoulli(jax.random.fold_in(key, 91), 0.5, (NG, 2, B))
    return jnp.where(flips, 1.0, -1.0).astype(jnp.float32)


def draw_stats_partial(key, part):
    key_noise = jax.random.fold_in(jax.random.fold_in(key, 11), 0)
    key_rows = jax.random.fold_in(jax.random.fold_in(key, 11), 2)
    key_blocks = jax.random.fold_in(jax.random.fold_in(key, 11), 3)
    key_weight = jax.random.fold_in(jax.random.fold_in(key, 11), 4)
    full_shape = (N_DP, NG, 2, B, B)
    noise_all = jnp.clip(jax.random.normal(key_noise, full_shape, jnp.float32), -6.0, 6.0)
    row_top = 0.5 * jnp.log(10.0)
    symmetric = (noise_all + jnp.swapaxes(noise_all, -1, -2)) * (0.35 / jnp.sqrt(2.0 * B))
    direction = shared_signs(key) / jnp.sqrt(1.0 * B)
    weight_dense = jax.random.uniform(key_weight, (N_DP, NG, 2, 1, 1), jnp.float32, 3.0, 8.0)
    dense_part = weight_dense * direction[None, :, :, :, None] * direction[None, :, :, None, :]
    base_matrix = symmetric + jnp.eye(B, dtype=jnp.float32) + dense_part
    row_scale = jnp.exp(jax.random.uniform(key_rows, (N_DP, NG, 2, B), jnp.float32, 0.0, row_top))
    block_scale = jnp.exp(jax.random.uniform(key_blocks, (1, NG, 2, 1, 1), jnp.float32, jnp.log(0.05), jnp.log(20.0)))
    return base_matrix * row_scale[..., :, None] * row_scale[..., None, :] * block_scale


def draw_gradient(key, part):
    key_noise = jax.random.fold_in(jax.random.fold_in(key, 23), 0)
    key_rows = jax.random.fold_in(jax.random.fold_in(key, 23), 2)
    key_cols = jax.random.fold_in(jax.random.fold_in(key, 23), 3)
    key_blocks = jax.random.fold_in(jax.random.fold_in(key, 23), 4)
    key_left = jax.random.fold_in(jax.random.fold_in(key, 23), 5)
    key_right = jax.random.fold_in(jax.random.fold_in(key, 23), 6)
    full_shape = (NG, B, B)
    noise_all = jnp.clip(jax.random.normal(key_noise, full_shape, jnp.float32), -5.5, 5.5)
    signs = shared_signs(key)
    column_mix = jnp.clip(jax.random.normal(key_left, (NG, B), jnp.float32), -2.5, 2.5)
    row_mix = jnp.clip(jax.random.normal(key_right, (NG, B), jnp.float32), -2.5, 2.5)
    aligned = signs[:, 0, :, None] * column_mix[:, None, :] + row_mix[:, :, None] * signs[:, 1, None, :]
    mixed = 0.7 * noise_all + 0.45 * aligned
    row_ramp = 1.0 + 2.0 * jnp.arange(B, dtype=jnp.float32) / (B - 1)
    row_scale = row_ramp[None, :] * jnp.exp(jax.random.uniform(key_rows, (NG, B), jnp.float32, jnp.log(0.7), jnp.log(1.4)))
    col_scale = jnp.exp(jax.random.uniform(key_cols, (NG, B), jnp.float32, 0.0, jnp.log(3.0)))
    block_scale = jnp.exp(jax.random.uniform(key_blocks, (NG, 1, 1), jnp.float32, -jnp.log(3.0), jnp.log(3.0)))
    return (mixed * row_scale[:, :, None] * col_scale[:, None, :] * block_scale).astype(jnp.bfloat16)


def draw_owner_of(key, part):
    key_heavy, key_rank, key_order = jax.random.split(jax.random.fold_in(key, 37), 3)
    slot_count = N_SHARD * OCAP
    heavy_owner = jax.random.randint(key_heavy, (), 0, N_SHARD)
    ranks = jax.random.permutation(key_rank, slot_count).astype(jnp.int32)
    places = jnp.arange(slot_count, dtype=jnp.int32)
    scores = jnp.where(places // OCAP == heavy_owner, places - slot_count, ranks)
    forced = (places == 0) | (places == (N_SHARD - 1) * OCAP)
    scores = jnp.where(forced, jnp.minimum(scores, -1), scores).astype(jnp.int32)
    ordered = jnp.argsort(scores, stable=True)
    owners = (ordered[:NG] // OCAP).astype(jnp.int32)
    return jnp.take(owners, jax.random.permutation(key_order, NG)).astype(jnp.int32)


def profile(count, total, reach, lean):
    loads = [(1 << 20) // math.isqrt(grade ** lean) + 1 for grade in range(2, count + 1)]
    surplus, counts = total - reach - (count - 1), [1] * (count - 1)
    while surplus > 0:
        free = [i for i in range(count - 1) if counts[i] < reach]
        mass, remaining = sum([loads[i] for i in free]), surplus
        for i in free:
            more = min(reach - counts[i], max(1, remaining * loads[i] // mass), surplus)
            counts[i] = counts[i] + more
            surplus = surplus - more
    return np.array([reach] + counts)


def ragged_sizes(rng, number_of, total, limit, lean):
    if number_of == 2:
        one = jax.random.randint(rng, (), max(1, total - limit), min(limit, total - 1) + 1)
        return jnp.stack([one, total - one])
    sizes = jnp.asarray(profile(number_of, total, limit, lean), jnp.int32)
    couples = (number_of - 1) // 2
    donor, receiver = sizes[1:1 + 2 * couples:2], sizes[2:2 + 2 * couples:2]
    slack = jnp.minimum(donor - 1, limit - receiver)
    moved = jax.random.randint(jax.random.fold_in(rng, 1), (couples,), 0, 1 << 20) % (slack + 1)
    sizes = sizes.at[1:1 + 2 * couples:2].set(donor - moved).at[2:2 + 2 * couples:2].set(receiver + moved)
    return sizes[jax.random.permutation(jax.random.fold_in(rng, 2), number_of)]


def setup_inputs(seed: int = 0) -> dict:
    splits = jax.random.split(jax.random.key(seed), 5)
    return {
        "stats_partial": draw_stats_partial(jax.random.fold_in(splits[4], 71), 0),
        "gradient": draw_gradient(jax.random.fold_in(splits[4], 71), 0),
        "owner_of": draw_owner_of(jax.random.fold_in(splits[4], 71), 0),
        "layer_count": ragged_sizes(splits[3], LAYERS, NG, NG // 2, 2).astype(jnp.int32),
    }


highest = lax.Precision.HIGHEST

def product(left_side, right_side):
    return jnp.dot(left_side, right_side, precision=highest, preferred_element_type=jnp.float32)

def inverse_root(statistic):
    identity = jnp.eye(B, dtype=jnp.float32)
    magnitude = B * jnp.sqrt(jnp.mean(statistic * statistic) + 1e-06)
    matrix = statistic / magnitude
    factor = identity * magnitude ** (-0.25)
    for number in range(ITERS):
        update = (5.0 * identity - matrix) * 0.25
        factor = product(factor, update)
        if number + 1 < ITERS:
            square = product(update, update)
            fourth = product(square, square)
            matrix = product(fourth, matrix)
    return factor.astype(jnp.bfloat16)

def per_block(inputs):
    stat_pair, grad_block = inputs
    left_factor = inverse_root(stat_pair[0])
    right_factor = inverse_root(stat_pair[1])
    middle = jnp.dot(left_factor, grad_block, preferred_element_type=jnp.float32).astype(jnp.bfloat16)
    raw_block = jnp.dot(middle, right_factor, preferred_element_type=jnp.float32)
    grad_wide = grad_block.astype(jnp.float32)
    return (raw_block, jnp.sum(grad_wide * grad_wide), jnp.sum(raw_block * raw_block))

def reference(stats_partial, gradient, owner_of, layer_count):
    statistics = lax.optimization_barrier(jnp.sum(stats_partial, axis=0))
    raw_all, grad_sq, raw_sq = lax.map(per_block, (statistics, gradient))
    blocks = gradient.shape[0]
    block_ids = jnp.arange(blocks, dtype=jnp.int32)
    layer_ends = jnp.cumsum(layer_count).astype(jnp.int32)
    layer_of = lax.optimization_barrier(jnp.sum((block_ids[:, None] >= layer_ends[None, :]).astype(jnp.int32), axis=1))
    layer_hot = (layer_of[:, None] == jnp.arange(LAYERS, dtype=jnp.int32)[None, :]).astype(jnp.float32)
    grad_norms = lax.optimization_barrier(jnp.sum(layer_hot * grad_sq[:, None], axis=0))
    raw_norms = lax.optimization_barrier(jnp.sum(layer_hot * raw_sq[:, None], axis=0))
    graft_ratio = jnp.sqrt((grad_norms + 1e-06) / (raw_norms + 1e-06))
    block_scale = lax.optimization_barrier(jnp.sum(layer_hot * graft_ratio[None, :], axis=1))
    scaled = (raw_all * block_scale[:, None, None]).astype(jnp.bfloat16)
    same_owner = (owner_of[:, None] == owner_of[None, :]) & (block_ids[None, :] < block_ids[:, None])
    earlier = lax.optimization_barrier(jnp.sum(same_owner.astype(jnp.int32), axis=1)).astype(jnp.int32)
    output = jnp.zeros((N_SHARD, OCAP, B, B), jnp.bfloat16)
    return output.at[owner_of.astype(jnp.int32), earlier].set(scaled)
```

```python
import functools

import jax
import jax.numpy as jnp
from jax import lax
from jax.experimental import pallas as pl
from jax.experimental.pallas import tpu as pltpu
from jax.sharding import Mesh
from jax.sharding import PartitionSpec as P

OCAP = 2
LAYERS = 4
LANES = 128
SHARD = ("z", "y", "c")
bf16, f32, i32 = jnp.bfloat16, jnp.float32, jnp.int32
SMEM = pl.BlockSpec(memory_space=pltpu.SMEM)
VMEM = pl.BlockSpec(memory_space=pltpu.VMEM)


def call(body, out_shape, in_specs, scratch=()):
    return pl.pallas_call(
        body,
        out_shape=out_shape,
        in_specs=in_specs,
        out_specs=jax.tree.map(lambda _: VMEM, out_shape),
        scratch_shapes=list(scratch),
    )


def packed(x):
    n, r, width = x.shape
    return x.reshape(n, r, 4, width // 4).transpose(0, 2, 1, 3).reshape(n, 4 * r, width // 4)


def pack_stats_body(order_ref, stats_ref, out_ref, *, groups, each, blocks):
    for x in range(groups):

        def step(k, carry, x=x):
            info = order_ref[k * groups + x]
            block = lax.rem(info, blocks)
            core = lax.rem(lax.div(info, blocks), 2)
            for c in range(2):
                out_ref[x * 2 + c, k] = stats_ref[2 * block + (core ^ c)].astype(bf16)
            return carry

        lax.fori_loop(0, each, step, 0, unroll=4)


def pack_grad_body(order_ref, place_ref, grad_ref, out_ref, *, groups, each, blocks):
    out_ref[...] = jnp.zeros(out_ref.shape, bf16)
    me = place_ref[0]

    def step(k, carry):
        info = order_ref[k * groups + me]
        column = lax.rem(lax.div(info, 2 * blocks), out_ref.shape[0])
        out_ref[column] = grad_ref[lax.rem(info, blocks)]
        return carry

    lax.fori_loop(0, each, step, 0, unroll=4)


def sum_stats_body(order_ref, place_ref, got_ref, out_ref, *, groups, each, blocks):
    out_ref[...] = jnp.zeros(out_ref.shape, bf16)
    me = place_ref[0]
    rows = got_ref.shape[2]

    def step(k, carry):
        column = lax.rem(lax.div(order_ref[k * groups + me], 2 * blocks), out_ref.shape[0])
        for c in range(2):
            total = got_ref[c, k].astype(f32)
            for x in range(1, groups):
                total = total + got_ref[2 * x + c, k].astype(f32)
            out_ref[column, c * rows : (c + 1) * rows] = total.astype(bf16)
        return carry

    lax.fori_loop(0, each, step, 0, unroll=4)


def dot(a, b):
    return jnp.dot(a, b, preferred_element_type=f32)


def newton_body(got_ref, out_ref, wide_ref, a_ref):
    order = out_ref.shape[0]
    chunk = got_ref.shape[2]
    wide_ref[...] = got_ref[...].astype(f32)
    for c in range(2):
        for q in range(4):
            a_ref[:, 4 * c : 4 * c + 4, q * chunk : (q + 1) * chunk] = wide_ref[
                :, 16 * c + 4 * q : 16 * c + 4 * q + 4, :
            ]
    a = a_ref[...].reshape(order, order)
    mean = jnp.sum(a * a, keepdims=True) * (1.0 / (order * order))
    magnitude = order * jnp.sqrt(mean + 1e-06)
    n = a * (0.25 / magnitude)
    nb = n.astype(bf16)
    e = dot(nb, nb) - 2.5 * n
    eb = e.astype(bf16)
    h = dot(eb, eb) + 3.125 * e
    n1 = dot(h.astype(bf16), nb) + 2.44140625 * n
    n1b = n1.astype(bf16)
    d = dot(nb, n1b) - 1.25 * (n + n1)
    e1 = dot(n1b, n1b) - 2.5 * n1
    e1b = e1.astype(bf16)
    h1 = dot(e1b, e1b) + 3.125 * e1
    n2 = dot(h1.astype(bf16), n1b) + 2.44140625 * n1
    x = 1.25 * d - 1.5625 * n2 - dot(d.astype(bf16), n2.astype(bf16))
    diagonal = lax.broadcasted_iota(i32, x.shape, 0) == lax.broadcasted_iota(i32, x.shape, 1)
    x = x + jnp.where(diagonal, 1.953125, 0.0)
    out_ref[...] = (x * (1.0 / jnp.sqrt(jnp.sqrt(magnitude)))).astype(bf16)


def raw_body(place_ref, factor_ref, other_ref, mine_ref, theirs_ref, out_ref, norm_ref, wide_ref, g_ref):
    order = factor_ref.shape[0]
    chunk = mine_ref.shape[2]
    quarter = order // out_ref.shape[0]
    core, live, is_left, layer = place_ref[1], place_ref[2], place_ref[3], place_ref[4]
    first = core == 0
    mine, theirs = mine_ref[...].astype(f32), theirs_ref[...].astype(f32)
    wide_ref[:, 0:16] = jnp.where(first, mine, theirs)
    wide_ref[:, 16:32] = jnp.where(first, theirs, mine)
    for c in range(2):
        for q in range(4):
            g_ref[:, 4 * c : 4 * c + 4, q * chunk : (q + 1) * chunk] = wide_ref[
                :, 16 * c + 4 * q : 16 * c + 4 * q + 4, :
            ]
    g = g_ref[...].reshape(order, order)
    gb = g.astype(bf16)
    grad_sq = jnp.sum(g * g, keepdims=True)
    lane = lax.broadcasted_iota(i32, (1, LANES), 1)

    def finish(left, right):
        middle = dot(left, gb).astype(bf16)
        raw = dot(middle, right)
        raw_sq = jnp.sum(raw * raw, keepdims=True)
        norms = jnp.where(lane == layer, grad_sq, 0.0) + jnp.where(lane == layer + LAYERS, raw_sq, 0.0)
        norms = jnp.where(live > 0, norms, 0.0)
        norm_ref[...] = jnp.broadcast_to(norms[:, None, :], norm_ref.shape)
        for x in range(out_ref.shape[0]):
            out_ref[x, 0:quarter] = raw[x * quarter : (x + 1) * quarter].astype(bf16)
            out_ref[x, quarter:] = jnp.zeros((out_ref.shape[1] - quarter, order), bf16)

    @pl.when(is_left > 0)
    def _():
        finish(factor_ref[...], other_ref[...])

    @pl.when(is_left == 0)
    def _():
        finish(other_ref[...], factor_ref[...])


def plane_body(norm_ref, raw_ref, out_ref):
    del raw_ref
    total = jnp.sum(norm_ref[...], axis=0)
    high = total.astype(bf16).astype(f32)
    mid = (total - high).astype(bf16).astype(f32)
    low = total - high - mid
    row = lax.broadcasted_iota(i32, (out_ref.shape[1], LANES), 0)
    tile = jnp.where(row == 0, high, 0.0) + jnp.where(row == 1, mid, 0.0) + jnp.where(row == 2, low, 0.0)
    for x in range(out_ref.shape[0]):
        out_ref[x] = jnp.zeros(out_ref.shape[1:], bf16)
        out_ref[x, :, 0:LANES] = tile.astype(bf16)


def scale_body(place_ref, got_ref, out_ref):
    quarter = out_ref.shape[1]
    total = jnp.zeros((1, LANES), f32)
    for x in range(got_ref.shape[0]):
        rows = got_ref[x, quarter:, 0:LANES].astype(f32)
        total = total + jnp.sum(rows, axis=0, keepdims=True)
    lane = lax.broadcasted_iota(i32, (1, LANES), 1)
    for s in range(OCAP):
        live, source, layer = place_ref[5 + 3 * s], place_ref[6 + 3 * s], place_ref[7 + 3 * s]
        grad_total = jnp.sum(jnp.where(lane == layer, total, 0.0), keepdims=True)
        raw_total = jnp.sum(jnp.where(lane == layer + LAYERS, total, 0.0), keepdims=True)
        ratio = jnp.sqrt((grad_total + 1e-06) / (raw_total + 1e-06))
        scaled = (got_ref[source, 0:quarter].astype(f32) * ratio).astype(bf16)
        out_ref[s] = jnp.where(live > 0, scaled, jnp.zeros((), bf16))


def on_device(stats_partial, gradient, owner_of, layer_count):
    groups = lax.axis_size("dp")
    columns = lax.axis_size("z") * lax.axis_size("y")
    x, c = lax.axis_index("dp"), lax.axis_index("c")
    column = lax.axis_index(("z", "y"))
    blocks = owner_of.shape[0]
    each = blocks // groups
    local_rows, order = gradient.shape[1:]
    quarter = order // groups
    chunk = order // 4

    ids = jnp.arange(blocks, dtype=i32)
    same = owner_of[None, :] == owner_of[:, None]
    before = ids[None, :] < ids[:, None]
    rank = jnp.sum(((owner_of[None, :] < owner_of[:, None]) | (same & before)).astype(i32), axis=1)
    slot = jnp.sum((same & before).astype(i32), axis=1)
    ends = jnp.cumsum(layer_count)
    layer = jnp.sum((ids[:, None] >= ends[None, :]).astype(i32), axis=1)
    info = ids + blocks * (owner_of + 2 * columns * (layer + LAYERS * slot))
    hit = rank[:, None] == ids[None, :]
    sorted_info = jnp.sum(jnp.where(hit, info[:, None], 0), axis=0)
    sorted_owner = lax.rem(lax.div(sorted_info, blocks), 2 * columns)
    group = lax.rem(ids, groups)

    def lookup(mask):
        found = jnp.sum(jnp.where(mask, sorted_info + blocks * 2 * columns * LAYERS * OCAP * (1 + group), 0))
        live = (found > 0).astype(i32)
        rest = lax.div(found, blocks * 2 * columns)
        source = jnp.maximum(lax.div(rest, LAYERS * OCAP) - 1, 0)
        return live, source, lax.rem(rest, LAYERS), lax.rem(lax.div(found, blocks), 2)

    mine = (lax.div(sorted_owner, 2) == column) & (group == x)
    live, _, my_layer, owner_core = lookup(mine)
    place = [x, c, live, (owner_core == c).astype(i32), my_layer]
    sorted_slot = lax.div(sorted_info, blocks * 2 * columns * LAYERS)
    for s in range(OCAP):
        place += list(lookup((sorted_owner == column * 2 + c) & (sorted_slot == s))[:3])
    place = jnp.stack(place).astype(i32)

    sizes = dict(groups=groups, each=each, blocks=blocks)
    struct = jax.ShapeDtypeStruct
    stats = packed(stats_partial.reshape(2 * blocks, local_rows, order))
    outgoing = call(
        functools.partial(pack_stats_body, **sizes),
        struct((2 * groups, each, 16, chunk), bf16),
        [SMEM, VMEM],
    )(sorted_info, stats)
    arrived = lax.all_to_all(outgoing, ("dp", "c"), 0, 0, tiled=True)

    grad_out = call(
        functools.partial(pack_grad_body, **sizes),
        struct((columns, 16, chunk), bf16),
        [SMEM, SMEM, VMEM],
    )(sorted_info, place, packed(gradient))
    grad_mine = lax.all_to_all(grad_out, ("z", "y"), 0, 0, tiled=True)
    grad_theirs = lax.ppermute(grad_mine, "c", [(0, 1), (1, 0)])

    summed = call(
        functools.partial(sum_stats_body, **sizes),
        struct((columns, 32, chunk), bf16),
        [SMEM, SMEM, VMEM],
    )(sorted_info, place, arrived)
    statistic = lax.all_to_all(summed, ("z", "y"), 0, 0, tiled=True)

    scratch = [pltpu.VMEM((columns, 32, chunk), f32), pltpu.VMEM((columns, 8, order), f32)]
    factor = call(newton_body, struct((order, order), bf16), [VMEM], scratch)(statistic)
    other = lax.ppermute(factor, "c", [(0, 1), (1, 0)])

    raw, norms = call(
        raw_body,
        (struct((groups, quarter + 8, order), bf16), struct((columns, 1, LANES), f32)),
        [SMEM, VMEM, VMEM, VMEM, VMEM],
        scratch,
    )(place, factor, other, grad_mine, grad_theirs)
    norms = lax.all_to_all(norms, ("z", "y"), 0, 0, tiled=True)
    tail = pl.BlockSpec((groups, 8, order), lambda i: (0, quarter // 8, 0))
    raw = pl.pallas_call(
        plane_body,
        grid=(1,),
        out_shape=struct(raw.shape, bf16),
        in_specs=[pl.BlockSpec(norms.shape, lambda i: (0, 0, 0)), pl.BlockSpec(memory_space=pl.ANY)],
        out_specs=tail,
        input_output_aliases={1: 0},
    )(norms, raw)
    spread = lax.all_to_all(raw, "dp", 0, 0, tiled=True)
    out = call(scale_body, struct((OCAP, quarter, order), bf16), [SMEM, VMEM])(place, spread)
    return out[None]


def solution(mesh):
    shards = mesh.shape["shard"]
    side = 1
    while (2 * side) ** 2 * 2 <= shards:
        side *= 2
    torus = Mesh(
        mesh.devices.reshape(mesh.shape["dp"], shards // (2 * side), side, 2), ("dp", "z", "y", "c")
    )
    placed = (P("dp", None, None, SHARD, None), P(None, SHARD, None), P(), P())
    return jax.shard_map(
        on_device,
        mesh=torus,
        in_specs=placed,
        out_specs=P(SHARD, None, "dp", None),
        check_vma=False,
    )
```

```python
import functools

import jax
import jax.numpy as jnp
from jax import lax
from jax.experimental import pallas as pl
from jax.experimental.pallas import tpu as pltpu
from jax.sharding import Mesh
from jax.sharding import PartitionSpec as P

OCAP = 2
LAYERS = 4
LANES = 128
SHARD = ("z", "y", "c")
bf16, f32, i32 = jnp.bfloat16, jnp.float32, jnp.int32
SMEM = pl.BlockSpec(memory_space=pltpu.SMEM)
VMEM = pl.BlockSpec(memory_space=pltpu.VMEM)


ANY = pl.BlockSpec(memory_space=pl.ANY)


def bits(size):
    assert size & (size - 1) == 0
    return size.bit_length() - 1


def call(body, out_shape, in_specs, scratch=()):
    return pl.pallas_call(
        body,
        out_shape=out_shape,
        in_specs=in_specs,
        out_specs=jax.tree.map(lambda _: VMEM, out_shape),
        scratch_shapes=list(scratch),
    )


def packed(x):
    n, r, width = x.shape
    return x.reshape(n, r, 4, width // 4).transpose(0, 2, 1, 3).reshape(n, 4 * r, width // 4)


def index_body(owner_ref, count_ref, sorted_ref, place_ref, *, groups, columns):
    blocks = owner_ref.shape[1]
    me_x, me_c, me_column = lax.axis_index("dp"), lax.axis_index("c"), lax.axis_index(("z", "y"))
    owner = owner_ref[...]
    row = jnp.broadcast_to(owner, (blocks, blocks))
    col = row.T
    sub = lax.broadcasted_iota(i32, row.shape, 0)
    lane = lax.broadcasted_iota(i32, row.shape, 1)
    same = (col == row) & (sub < lane)
    rank = jnp.sum(jnp.where((col < row) | same, 1, 0), axis=0, keepdims=True)
    slot = jnp.sum(jnp.where(same, 1, 0), axis=0, keepdims=True)
    one_lane = lax.broadcasted_iota(i32, owner.shape, 1)
    layer = jnp.zeros(owner.shape, i32)
    end = jnp.int32(0)
    for number in range(LAYERS - 1):
        end = end + count_ref[number]
        layer = layer + jnp.where(one_lane >= end, 1, 0)
    owner_at = bits(blocks)
    layer_at = owner_at + bits(2 * columns)
    slot_at = layer_at + bits(LAYERS)
    top = slot_at + bits(OCAP)
    info = one_lane + (owner << owner_at) + (layer << layer_at) + (slot << slot_at)
    both = jnp.broadcast_to(info + (rank << top), row.shape).T
    ordered = jnp.sum(
        jnp.where((both >> top) == lane, both & ((1 << top) - 1), 0), axis=0, keepdims=True
    )
    sorted_ref[...] = ordered
    ordered_owner = (ordered >> owner_at) & (2 * columns - 1)
    group = one_lane & (groups - 1)
    coded = ordered + ((group + 1) << top)

    def lookup(mask):
        found = jnp.sum(jnp.where(mask, coded, 0), axis=1, keepdims=True)
        live = jnp.where(found > 0, 1, 0)
        source = jnp.maximum((found >> top) - 1, 0)
        return live, source, (found >> layer_at) & (LAYERS - 1), (found >> owner_at) & 1

    live, _, my_layer, core = lookup(((ordered_owner >> 1) == me_column) & (group == me_x))
    place = [live, core, my_layer]
    for s in range(OCAP):
        mask = (ordered_owner == me_column * 2 + me_c) & ((ordered >> slot_at) == s)
        place += list(lookup(mask)[:3])
    wide = lax.broadcasted_iota(i32, place_ref.shape, 1)
    out = jnp.zeros(place_ref.shape, i32)
    for number, value in enumerate(place):
        out = jnp.where(wide == number, value, out)
    place_ref[...] = out


def pack_stats_body(
    owner_ref, count_ref, stats_ref, out_ref, sorted_ref, place_ref, stats_vmem, out_vmem, order_ref, sems, *, groups, columns
):
    blocks = owner_ref.shape[1]
    each = out_ref.shape[1]
    load = pltpu.make_async_copy(stats_ref, stats_vmem, sems.at[0])
    load.start()
    index_body(owner_ref, count_ref, sorted_ref, place_ref, groups=groups, columns=columns)
    move = pltpu.make_async_copy(sorted_ref, order_ref, sems.at[1])
    move.start()
    move.wait()
    load.wait()
    stores = []
    for x in range(groups):

        def step(k, carry, x=x):
            info = order_ref[0, k * groups + x]
            block = info & (blocks - 1)
            core = (info >> bits(blocks)) & 1
            for c in range(2):
                out_vmem[x * 2 + c, k] = stats_vmem[2 * block + (core ^ c)].astype(bf16)
            return carry

        lax.fori_loop(0, each, step, 0, unroll=8 if each % 8 == 0 else 1)
        part = slice(2 * x, 2 * x + 2)
        stores.append(pltpu.make_async_copy(out_vmem.at[part], out_ref.at[part], sems.at[2 + x]))
        stores[-1].start()
    for store in stores:
        store.wait()


def grad_half_body(order_ref, grad_ref, out_ref, *, groups, blocks):
    me = lax.axis_index("dp")
    at = 8 * (1 - lax.axis_index("c"))

    def step(k, carry):
        block = order_ref[0, k * groups + me] & (blocks - 1)
        out_ref[k] = grad_ref[block, pl.ds(pl.multiple_of(at, 8), 8), :]
        return carry

    each = blocks // groups
    lax.fori_loop(0, each, step, 0, unroll=8 if each % 8 == 0 else 1)


def joined(first, second):
    top = lax.broadcasted_iota(i32, first.shape, 0) < 4
    even = jnp.where(top, first, pltpu.roll(second, 4, 0))
    odd = jnp.where(top, pltpu.roll(first, 4, 0), second)
    return even, odd


def sum_stats_body(order_ref, got_ref, grad_ref, theirs_ref, out_ref, *, groups, blocks):
    out_ref[...] = jnp.zeros(out_ref.shape, bf16)
    me = lax.axis_index("dp")
    core = lax.axis_index("c")

    def step(k, carry):
        info = order_ref[0, k * groups + me]
        column = (info >> (bits(blocks) + 1)) & (out_ref.shape[0] - 1)
        sums = []
        for c in range(2):
            total = got_ref[c, k].astype(f32)
            for x in range(1, groups):
                total = total + got_ref[2 * x + c, k].astype(f32)
            sums.append(total)
        tiles = []
        for v in range(2):
            tiles += joined(sums[0][8 * v : 8 * v + 8], sums[1][8 * v : 8 * v + 8])
        mine = grad_ref[info & (blocks - 1), pl.ds(pl.multiple_of(8 * core, 8), 8), :].astype(f32)
        theirs = theirs_ref[k].astype(f32)
        tiles += joined(jnp.where(core == 0, mine, theirs), jnp.where(core == 0, theirs, mine))
        for v in range(3):
            pair = jnp.concatenate(tiles[2 * v : 2 * v + 2], axis=0)
            out_ref[column, 16 * v : 16 * v + 16] = pair.astype(bf16)
        return carry

    each = blocks // groups
    lax.fori_loop(0, each, step, 0, unroll=4 if each % 4 == 0 else 1)


def dot(a, b):
    return jnp.dot(a, b, preferred_element_type=f32)


def newton_body(got_ref, out_ref, a_ref):
    order = out_ref.shape[1]
    chunk = got_ref.shape[2]
    for q in range(4):
        tile = got_ref[:, 8 * q : 8 * q + 8, :].astype(f32).reshape(order, chunk)
        a_ref[:, q * chunk : (q + 1) * chunk] = tile
    for q in range(2):
        tile = got_ref[:, 32 + 8 * q : 40 + 8 * q, :].astype(f32).reshape(order, chunk).astype(bf16)
        for v in range(2):
            place = slice((2 * v + q) * chunk, (2 * v + q + 1) * chunk)
            out_ref[order:, place] = tile[v * order // 2 : (v + 1) * order // 2]
    a = a_ref[...]
    mean = jnp.sum(a * a, keepdims=True) * (1.0 / (order * order))
    magnitude = order * jnp.sqrt(mean + 1e-06)
    n = a * (0.25 / magnitude)
    nb = n.astype(bf16)
    e = dot(nb, nb) - 2.5 * n
    eb = e.astype(bf16)
    h = dot(eb, eb) + 3.125 * e
    n1 = dot(h.astype(bf16), nb) + 2.44140625 * n
    n1b = n1.astype(bf16)
    d = dot(nb, n1b) - 1.25 * (n + n1)
    e1 = dot(n1b, n1b) - 2.5 * n1
    e1b = e1.astype(bf16)
    h1 = dot(e1b, e1b) + 3.125 * e1
    n2 = dot(h1.astype(bf16), n1b) + 2.44140625 * n1
    x = 1.25 * d - 1.5625 * n2 - dot(d.astype(bf16), n2.astype(bf16))
    diagonal = lax.broadcasted_iota(i32, x.shape, 0) == lax.broadcasted_iota(i32, x.shape, 1)
    x = x + jnp.where(diagonal, 1.953125, 0.0)
    out_ref[0:order] = (x * (1.0 / jnp.sqrt(jnp.sqrt(magnitude)))).astype(bf16)


def raw_body(place_ref, mine_ref, other_ref, out_ref, norm_ref, both_ref, sems):
    quarter = out_ref.shape[1]
    order = mine_ref.shape[1]
    half = order // 2
    live, core, layer = place_ref[0, 0], place_ref[0, 1], place_ref[0, 2]
    me_c, me_x = lax.axis_index("c"), lax.axis_index("dp")
    loads = [
        pltpu.make_async_copy(mine_ref, both_ref.at[me_c], sems.at[0]),
        pltpu.make_async_copy(other_ref, both_ref.at[1 - me_c], sems.at[1]),
    ]
    for load in loads:
        load.start()
    for load in loads:
        load.wait()
    raw = jnp.zeros((order, order), f32)
    grad_sq = jnp.zeros((1, 1), f32)
    for c in range(2):
        middle = jnp.zeros((order, half), f32)
        for v in range(2):
            grad = both_ref[c, order:, v * half : (v + 1) * half]
            middle = middle + dot(both_ref[core, 0:order, v * half : (v + 1) * half], grad)
            wide = grad.astype(f32)
            grad_sq = grad_sq + jnp.sum(wide * wide, keepdims=True)
        raw = raw + dot(middle.astype(bf16), both_ref[1 - core, c * half : (c + 1) * half])
    raw_sq = jnp.sum(raw * raw, keepdims=True)
    lane = lax.broadcasted_iota(i32, (1, LANES), 1)
    norms = jnp.where(lane == layer, grad_sq, 0.0) + jnp.where(lane == layer + LAYERS, raw_sq, 0.0)
    norms = jnp.where(live > 0, norms, 0.0)
    norm_ref[...] = jnp.broadcast_to(norms[:, None, :], norm_ref.shape)
    groups = out_ref.shape[0]
    for x in range(groups):
        out_ref[(x - me_x) & (groups - 1)] = raw[x * quarter : (x + 1) * quarter].astype(bf16)


def scale_body(place_ref, norm_ref, raw_ref, *refs):
    out_ref = refs[-1]
    groups = len(refs)
    total = jnp.sum(norm_ref[...], axis=0)
    lane = lax.broadcasted_iota(i32, (1, LANES), 1)
    me_x = lax.axis_index("dp")
    for s in range(OCAP):
        live, source, layer = place_ref[0, 3 + 3 * s], place_ref[0, 4 + 3 * s], place_ref[0, 5 + 3 * s]
        grad_total = jnp.sum(jnp.where(lane == layer, total, 0.0), keepdims=True)
        raw_total = jnp.sum(jnp.where(lane == layer + LAYERS, total, 0.0), keepdims=True)
        ratio = jnp.sqrt((grad_total + 1e-06) / (raw_total + 1e-06))
        ratio = jnp.where(live > 0, ratio, 0.0)
        step = jnp.where(live > 0, (me_x - source) & (groups - 1), groups)
        for number in range(groups):

            @pl.when(step == number)
            def _(number=number, s=s, ratio=ratio):
                block = raw_ref[0] if number == 0 else refs[number - 1][0]
                out_ref[s] = (block.astype(f32) * ratio).astype(bf16)

        @pl.when(step == groups)
        def _(s=s):
            out_ref[s] = jnp.zeros(out_ref.shape[1:], bf16)


def on_device(stats_partial, gradient, owner_of, layer_count):
    groups = lax.axis_size("dp")
    columns = lax.axis_size("z") * lax.axis_size("y")
    blocks = owner_of.shape[0]
    each = blocks // groups
    local_rows, order = gradient.shape[1:]
    quarter = order // groups
    chunk = order // 4
    struct = jax.ShapeDtypeStruct
    swap = [(0, 1), (1, 0)]

    stats = packed(stats_partial.reshape(2 * blocks, local_rows, order))
    out_shape = (2 * groups, each, 16, chunk)
    outgoing, order_info, place = pl.pallas_call(
        functools.partial(pack_stats_body, groups=groups, columns=columns),
        out_shape=(struct(out_shape, bf16), struct((1, blocks), i32), struct((1, 128), i32)),
        in_specs=[VMEM, SMEM, ANY],
        out_specs=(ANY, VMEM, VMEM),
        scratch_shapes=[
            pltpu.VMEM(stats.shape, f32),
            pltpu.VMEM(out_shape, bf16),
            pltpu.SMEM((1, blocks), i32),
            pltpu.SemaphoreType.DMA((2 + groups,)),
        ],
    )(owner_of[None], layer_count, stats)
    arrived = lax.all_to_all(outgoing, ("dp", "c"), 0, 0, tiled=True)
    grad = packed(gradient)
    grad_half = call(
        functools.partial(grad_half_body, groups=groups, blocks=blocks),
        struct((each, 8, chunk), bf16),
        [SMEM, VMEM],
    )(order_info, grad)
    grad_theirs = lax.ppermute(grad_half, "c", swap)
    summed = call(
        functools.partial(sum_stats_body, groups=groups, blocks=blocks),
        struct((columns, 48, chunk), bf16),
        [SMEM, VMEM, VMEM, VMEM],
    )(order_info, arrived, grad, grad_theirs)
    statistic = lax.all_to_all(summed, ("z", "y"), 0, 0, tiled=True)
    bundle_shape = (order + order // 2, order)
    bundle = call(
        newton_body, struct(bundle_shape, bf16), [VMEM], [pltpu.VMEM((order, order), f32)]
    )(statistic)
    other = lax.ppermute(bundle, "c", swap)
    raw, norms = call(
        raw_body,
        (struct((groups, quarter, order), bf16), struct((groups * columns, 1, LANES), f32)),
        [SMEM, ANY, ANY],
        [pltpu.VMEM((2, *bundle_shape), bf16), pltpu.SemaphoreType.DMA((2,))],
    )(place, bundle, other)
    norms = lax.all_to_all(norms, ("dp", "z", "y"), 0, 0, tiled=True)
    spread = []
    for step in range(1, groups):
        pairs = [(i, (i + step) % groups) for i in range(groups)]
        spread.append(lax.ppermute(raw[step : step + 1], "dp", pairs))
    own = raw[0:1]
    out = call(
        scale_body, struct((OCAP, quarter, order), bf16), [SMEM, VMEM] + [VMEM] * groups
    )(place, norms, own, *spread)
    return out[None]


def solution(mesh):
    shards = mesh.shape["shard"]
    side = 1
    while (2 * side) ** 2 * 2 <= shards:
        side *= 2
    torus = Mesh(
        mesh.devices.reshape(mesh.shape["dp"], shards // (2 * side), side, 2), ("dp", "z", "y", "c")
    )
    placed = (P("dp", None, None, SHARD, None), P(None, SHARD, None), P(), P())
    return jax.shard_map(
        on_device,
        mesh=torus,
        in_specs=placed,
        out_specs=P(SHARD, None, "dp", None),
        check_vma=False,
    )
```

```python
import functools

import jax
import jax.numpy as jnp
from jax import lax
from jax.experimental import pallas as pl
from jax.experimental.pallas import tpu as pltpu
from jax.sharding import Mesh
from jax.sharding import PartitionSpec as P

OCAP = 2
LAYERS = 4
LANES = 128
SHARD = ("z", "y", "c")
bf16, f32, i32 = jnp.bfloat16, jnp.float32, jnp.int32
SMEM = pl.BlockSpec(memory_space=pltpu.SMEM)
VMEM = pl.BlockSpec(memory_space=pltpu.VMEM)


ANY = pl.BlockSpec(memory_space=pl.ANY)


def bits(size):
    assert size & (size - 1) == 0
    return size.bit_length() - 1


def held(x):
    return pltpu.with_memory_space_constraint(x, pltpu.VMEM)


def in_hbm(x):
    return pltpu.with_memory_space_constraint(x, pltpu.HBM)


def call(body, out_shape, in_specs, scratch=(), out_specs=None):
    return pl.pallas_call(
        body,
        out_shape=out_shape,
        in_specs=in_specs,
        out_specs=VMEM if out_specs is None else out_specs,
        scratch_shapes=list(scratch),
        compiler_params=pltpu.CompilerParams(vmem_limit_bytes=24 * 2**20),
    )


def packed(x):
    n, r, width = x.shape
    return x.reshape(n, r, 4, width // 4).transpose(0, 2, 1, 3).reshape(n, 4 * r, width // 4)


def index_body(owner_ref, count_ref, sorted_ref, place_ref, *, groups, columns):
    blocks = owner_ref.shape[1]
    me_x, me_c, me_column = lax.axis_index("dp"), lax.axis_index("c"), lax.axis_index(("z", "y"))
    owner = owner_ref[...]
    row = jnp.broadcast_to(owner, (blocks, blocks))
    col = row.T
    sub = lax.broadcasted_iota(i32, row.shape, 0)
    lane = lax.broadcasted_iota(i32, row.shape, 1)
    same = (col == row) & (sub < lane)
    rank = jnp.sum(jnp.where((col < row) | same, 1, 0), axis=0, keepdims=True)
    slot = jnp.sum(jnp.where(same, 1, 0), axis=0, keepdims=True)
    one_lane = lax.broadcasted_iota(i32, owner.shape, 1)
    layer = jnp.zeros(owner.shape, i32)
    end = jnp.int32(0)
    for number in range(LAYERS - 1):
        end = end + count_ref[number]
        layer = layer + jnp.where(one_lane >= end, 1, 0)
    owner_at = bits(blocks)
    layer_at = owner_at + bits(2 * columns)
    slot_at = layer_at + bits(LAYERS)
    top = slot_at + bits(OCAP)
    info = one_lane + (owner << owner_at) + (layer << layer_at) + (slot << slot_at)
    both = jnp.broadcast_to(info + (rank << top), row.shape).T
    ordered = jnp.sum(
        jnp.where((both >> top) == lane, both & ((1 << top) - 1), 0), axis=0, keepdims=True
    )
    sorted_ref[...] = ordered
    ordered_owner = (ordered >> owner_at) & (2 * columns - 1)
    group = one_lane & (groups - 1)
    coded = ordered + ((group + 1) << top)

    def lookup(mask):
        found = jnp.sum(jnp.where(mask, coded, 0), axis=1, keepdims=True)
        live = jnp.where(found > 0, 1, 0)
        source = jnp.maximum((found >> top) - 1, 0)
        return live, source, (found >> layer_at) & (LAYERS - 1), (found >> owner_at) & 1

    live, _, my_layer, core = lookup(((ordered_owner >> 1) == me_column) & (group == me_x))
    place = [live, core, my_layer]
    for s in range(OCAP):
        mask = (ordered_owner == me_column * 2 + me_c) & ((ordered >> slot_at) == s)
        place += list(lookup(mask)[:3])
    wide = lax.broadcasted_iota(i32, place_ref.shape, 1)
    out = jnp.zeros(place_ref.shape, i32)
    for number, value in enumerate(place):
        out = jnp.where(wide == number, value, out)
    place_ref[...] = out


def pack_stats_body(
    owner_ref, count_ref, stats_ref, out_ref, sorted_ref, place_ref, stats_vmem, order_ref, sems, *, groups, columns
):
    blocks = owner_ref.shape[1]
    each = out_ref.shape[1]
    load = pltpu.make_async_copy(stats_ref, stats_vmem, sems.at[0])
    load.start()
    index_body(owner_ref, count_ref, sorted_ref, place_ref, groups=groups, columns=columns)
    move = pltpu.make_async_copy(sorted_ref, order_ref, sems.at[1])
    move.start()
    move.wait()
    load.wait()
    for x in range(groups):

        def step(k, carry, x=x):
            info = order_ref[0, k * groups + x]
            block = info & (blocks - 1)
            core = (info >> bits(blocks)) & 1
            for c in range(2):
                out_ref[x * 2 + c, k] = stats_vmem[2 * block + (core ^ c)].astype(bf16)
            return carry

        lax.fori_loop(0, each, step, 0, unroll=8 if each % 8 == 0 else 1)


def grad_half_body(order_ref, grad_ref, out_ref, *, groups, blocks):
    me = lax.axis_index("dp")
    at = 8 * (1 - lax.axis_index("c"))

    def step(k, carry):
        block = order_ref[0, k * groups + me] & (blocks - 1)
        out_ref[k] = grad_ref[block, pl.ds(pl.multiple_of(at, 8), 8), :]
        return carry

    each = blocks // groups
    lax.fori_loop(0, each, step, 0, unroll=8 if each % 8 == 0 else 1)


def joined(first, second):
    top = lax.broadcasted_iota(i32, first.shape, 0) < 4
    even = jnp.where(top, first, pltpu.roll(second, 4, 0))
    odd = jnp.where(top, pltpu.roll(first, 4, 0), second)
    return even, odd


def sum_stats_body(order_ref, got_ref, grad_ref, theirs_ref, out_ref, *, groups, blocks):
    out_ref[...] = jnp.zeros(out_ref.shape, bf16)
    me = lax.axis_index("dp")
    core = lax.axis_index("c")

    def step(k, carry):
        info = order_ref[0, k * groups + me]
        column = (info >> (bits(blocks) + 1)) & (out_ref.shape[0] - 1)
        sums = []
        for c in range(2):
            total = got_ref[c, k].astype(f32)
            for x in range(1, groups):
                total = total + got_ref[2 * x + c, k].astype(f32)
            sums.append(total)
        tiles = []
        for v in range(2):
            tiles += joined(sums[0][8 * v : 8 * v + 8], sums[1][8 * v : 8 * v + 8])
        mine = grad_ref[info & (blocks - 1), pl.ds(pl.multiple_of(8 * core, 8), 8), :].astype(f32)
        theirs = theirs_ref[k].astype(f32)
        tiles += joined(jnp.where(core == 0, mine, theirs), jnp.where(core == 0, theirs, mine))
        for v in range(3):
            pair = jnp.concatenate(tiles[2 * v : 2 * v + 2], axis=0)
            out_ref[column, 16 * v : 16 * v + 16] = pair.astype(bf16)
        return carry

    each = blocks // groups
    lax.fori_loop(0, each, step, 0, unroll=4 if each % 4 == 0 else 1)


def dot(a, b):
    return jnp.dot(a, b, preferred_element_type=f32)


def newton_body(got_ref, out_ref, a_ref):
    order = out_ref.shape[1]
    chunk = got_ref.shape[2]
    for q in range(4):
        tile = got_ref[:, 8 * q : 8 * q + 8, :].astype(f32).reshape(order, chunk)
        a_ref[:, q * chunk : (q + 1) * chunk] = tile
    for q in range(2):
        tile = got_ref[:, 32 + 8 * q : 40 + 8 * q, :].astype(f32).reshape(order, chunk).astype(bf16)
        for v in range(2):
            place = slice((2 * v + q) * chunk, (2 * v + q + 1) * chunk)
            out_ref[order:, place] = tile[v * order // 2 : (v + 1) * order // 2]
    a = a_ref[...]
    mean = jnp.sum(a * a, keepdims=True) * (1.0 / (order * order))
    magnitude = order * jnp.sqrt(mean + 1e-06)
    n = a * (0.25 / magnitude)
    nb = n.astype(bf16)
    e = dot(nb, nb) - 2.5 * n
    eb = e.astype(bf16)
    h = dot(eb, eb) + 3.125 * e
    n1 = dot(h.astype(bf16), nb) + 2.44140625 * n
    n1b = n1.astype(bf16)
    d = dot(nb, n1b) - 1.25 * (n + n1)
    e1 = dot(n1b, n1b) - 2.5 * n1
    e1b = e1.astype(bf16)
    h1 = dot(e1b, e1b) + 3.125 * e1
    n2 = dot(h1.astype(bf16), n1b) + 2.44140625 * n1
    x = 1.25 * d - 1.5625 * n2 - dot(d.astype(bf16), n2.astype(bf16))
    diagonal = lax.broadcasted_iota(i32, x.shape, 0) == lax.broadcasted_iota(i32, x.shape, 1)
    x = x + jnp.where(diagonal, 1.953125, 0.0)
    out_ref[0:order] = (x * (1.0 / jnp.sqrt(jnp.sqrt(magnitude)))).astype(bf16)


def raw_body(place_ref, mine_ref, other_ref, *refs):
    norm_ref, both_ref, raw_ref, sems = refs[-4:]
    out_refs = refs[:-4]
    groups = len(out_refs)
    order = mine_ref.shape[1]
    half, quarter = order // 2, order // groups
    live, core, layer = place_ref[0, 0], place_ref[0, 1], place_ref[0, 2]
    me_c, me_x = lax.axis_index("c"), lax.axis_index("dp")
    loads = [
        pltpu.make_async_copy(mine_ref, both_ref.at[me_c], sems.at[0]),
        pltpu.make_async_copy(other_ref, both_ref.at[1 - me_c], sems.at[1]),
    ]
    for load in loads:
        load.start()
    for load in loads:
        load.wait()
    raw = jnp.zeros((order, order), f32)
    grad_sq = jnp.zeros((1, 1), f32)
    for c in range(2):
        middle = jnp.zeros((order, half), f32)
        for v in range(2):
            grad = both_ref[c, order:, v * half : (v + 1) * half]
            middle = middle + dot(both_ref[core, 0:order, v * half : (v + 1) * half], grad)
            wide = grad.astype(f32)
            grad_sq = grad_sq + jnp.sum(wide * wide, keepdims=True)
        raw = raw + dot(middle.astype(bf16), both_ref[1 - core, c * half : (c + 1) * half])
    raw_sq = jnp.sum(raw * raw, keepdims=True)
    lane = lax.broadcasted_iota(i32, (1, LANES), 1)
    norms = jnp.where(lane == layer, grad_sq, 0.0) + jnp.where(lane == layer + LAYERS, raw_sq, 0.0)
    norms = jnp.where(live > 0, norms, 0.0)
    norm_ref[...] = jnp.broadcast_to(norms[:, None, :], norm_ref.shape)
    raw_ref[...] = raw.astype(bf16)
    for number, out_ref in enumerate(out_refs):
        start = ((me_x + number) & (groups - 1)) * quarter
        out_ref[...] = raw_ref[pl.ds(pl.multiple_of(start, quarter), quarter), :]


def scale_body(place_ref, norm_ref, raw_ref, *refs):
    out_ref = refs[-1]
    groups = len(refs)
    total = jnp.sum(norm_ref[...], axis=0)
    lane = lax.broadcasted_iota(i32, (1, LANES), 1)
    me_x = lax.axis_index("dp")
    for s in range(OCAP):
        live, source, layer = place_ref[0, 3 + 3 * s], place_ref[0, 4 + 3 * s], place_ref[0, 5 + 3 * s]
        grad_total = jnp.sum(jnp.where(lane == layer, total, 0.0), keepdims=True)
        raw_total = jnp.sum(jnp.where(lane == layer + LAYERS, total, 0.0), keepdims=True)
        ratio = jnp.sqrt((grad_total + 1e-06) / (raw_total + 1e-06))
        ratio = jnp.where(live > 0, ratio, 0.0)
        step = jnp.where(live > 0, (me_x - source) & (groups - 1), groups)
        for number in range(groups):

            @pl.when(step == number)
            def _(number=number, s=s, ratio=ratio):
                block = raw_ref[...] if number == 0 else refs[number - 1][...]
                out_ref[s] = (block.astype(f32) * ratio).astype(bf16)

        @pl.when(step == groups)
        def _(s=s):
            out_ref[s] = jnp.zeros(out_ref.shape[1:], bf16)


def on_device(stats_partial, gradient, owner_of, layer_count):
    groups = lax.axis_size("dp")
    columns = lax.axis_size("z") * lax.axis_size("y")
    blocks = owner_of.shape[0]
    each = blocks // groups
    local_rows, order = gradient.shape[1:]
    quarter = order // groups
    chunk = order // 4
    struct = jax.ShapeDtypeStruct
    swap = [(0, 1), (1, 0)]

    stats = packed(stats_partial.reshape(2 * blocks, local_rows, order))
    out_shape = (2 * groups, each, 16, chunk)
    outgoing, order_info, place = call(
        functools.partial(pack_stats_body, groups=groups, columns=columns),
        (pltpu.VMEM(out_shape, bf16), struct((1, blocks), i32), struct((1, 128), i32)),
        [VMEM, SMEM, ANY],
        [
            pltpu.VMEM(stats.shape, f32),
            pltpu.SMEM((1, blocks), i32),
            pltpu.SemaphoreType.DMA((2,)),
        ],
        (VMEM, VMEM, VMEM),
    )(in_hbm(owner_of[None]), in_hbm(layer_count), in_hbm(stats))
    arrived = lax.all_to_all(outgoing, ("dp", "c"), 0, 0, tiled=True)
    grad = packed(gradient)
    grad_half = call(
        functools.partial(grad_half_body, groups=groups, blocks=blocks),
        pltpu.VMEM((each, 8, chunk), bf16),
        [SMEM, VMEM],
    )(order_info, grad)
    grad_theirs = lax.ppermute(grad_half, "c", swap)
    summed = call(
        functools.partial(sum_stats_body, groups=groups, blocks=blocks),
        pltpu.VMEM((columns, 48, chunk), bf16),
        [SMEM, VMEM, VMEM, VMEM],
    )(order_info, held(arrived), grad, held(grad_theirs))
    statistic = lax.all_to_all(summed, ("z", "y"), 0, 0, tiled=True)
    bundle_shape = (order + order // 2, order)
    bundle = call(
        newton_body, pltpu.VMEM(bundle_shape, bf16), [VMEM], [pltpu.VMEM((order, order), f32)]
    )(held(statistic))
    other = lax.ppermute(bundle, "c", swap)
    *quarters, norms = call(
        raw_body,
        tuple(pltpu.VMEM((quarter, order), bf16) for _ in range(groups))
        + (pltpu.VMEM((groups * columns, 1, LANES), f32),),
        [SMEM, ANY, ANY],
        [
            pltpu.VMEM((2, *bundle_shape), bf16),
            pltpu.VMEM((order, order), bf16),
            pltpu.SemaphoreType.DMA((2,)),
        ],
        (VMEM,) * (groups + 1),
    )(place, held(bundle), held(other))
    norms = lax.all_to_all(norms, ("dp", "z", "y"), 0, 0, tiled=True)
    spread = [held(quarters[0])]
    for step in range(1, groups):
        pairs = [(i, (i + step) % groups) for i in range(groups)]
        spread.append(held(lax.ppermute(quarters[step], "dp", pairs)))
    out = call(
        scale_body, struct((OCAP, quarter, order), bf16), [SMEM] + [VMEM] * (groups + 1)
    )(place, held(norms), *spread)
    return out[None]


def solution(mesh):
    shards = mesh.shape["shard"]
    side = 1
    while (2 * side) ** 2 * 2 <= shards:
        side *= 2
    torus = Mesh(
        mesh.devices.reshape(mesh.shape["dp"], shards // (2 * side), side, 2), ("dp", "z", "y", "c")
    )
    placed = (P("dp", None, None, SHARD, None), P(None, SHARD, None), P(), P())
    return jax.shard_map(
        on_device,
        mesh=torus,
        in_specs=placed,
        out_specs=P(SHARD, None, "dp", None),
        check_vma=False,
    )
```

```python
import functools

import jax
import jax.numpy as jnp
from jax import lax
from jax.experimental import pallas as pl
from jax.experimental.pallas import tpu as pltpu
from jax.sharding import Mesh
from jax.sharding import PartitionSpec as P

OCAP = 2
LAYERS = 4
LANES = 128
SHARD = ("z", "y", "c")
bf16, f32, i32 = jnp.bfloat16, jnp.float32, jnp.int32
SMEM = pl.BlockSpec(memory_space=pltpu.SMEM)
VMEM = pl.BlockSpec(memory_space=pltpu.VMEM)


ANY = pl.BlockSpec(memory_space=pl.ANY)


def bits(size):
    assert size & (size - 1) == 0
    return size.bit_length() - 1


def held(x):
    return pltpu.with_memory_space_constraint(x, pltpu.VMEM)


def in_hbm(x):
    return pltpu.with_memory_space_constraint(x, pltpu.HBM)


def call(body, out_shape, in_specs, scratch=(), out_specs=None):
    return pl.pallas_call(
        body,
        out_shape=out_shape,
        in_specs=in_specs,
        out_specs=VMEM if out_specs is None else out_specs,
        scratch_shapes=list(scratch),
        compiler_params=pltpu.CompilerParams(vmem_limit_bytes=24 * 2**20),
    )


def packed(x):
    n, r, width = x.shape
    return x.reshape(n, r, 4, width // 4).transpose(0, 2, 1, 3).reshape(n, 4 * r, width // 4)


SINGLE = (3, 2, 0, 1)
MISSING = (2, 3, 1, 0)


def joined(first, second):
    top = lax.broadcasted_iota(i32, first.shape, 0) < 4
    even = jnp.where(top, first, pltpu.roll(second, 4, 0))
    odd = jnp.where(top, pltpu.roll(first, 4, 0), second)
    return even, odd


def index_body(owner_ref, count_ref, sorted_ref, place_ref, *, groups, columns):
    blocks = owner_ref.shape[1]
    me_x, me_c, me_column = lax.axis_index("dp"), lax.axis_index("c"), lax.axis_index(("z", "y"))
    owner = owner_ref[...]
    row = jnp.broadcast_to(owner, (blocks, blocks))
    col = row.T
    sub = lax.broadcasted_iota(i32, row.shape, 0)
    lane = lax.broadcasted_iota(i32, row.shape, 1)
    same = (col == row) & (sub < lane)
    rank = jnp.sum(jnp.where((col < row) | same, 1, 0), axis=0, keepdims=True)
    slot = jnp.sum(jnp.where(same, 1, 0), axis=0, keepdims=True)
    one_lane = lax.broadcasted_iota(i32, owner.shape, 1)
    layer = jnp.zeros(owner.shape, i32)
    end = jnp.int32(0)
    for number in range(LAYERS - 1):
        end = end + count_ref[number]
        layer = layer + jnp.where(one_lane >= end, 1, 0)
    owner_at = bits(blocks)
    layer_at = owner_at + bits(2 * columns)
    slot_at = layer_at + bits(LAYERS)
    top = slot_at + bits(OCAP)
    info = one_lane + (owner << owner_at) + (layer << layer_at) + (slot << slot_at)
    both = jnp.broadcast_to(info + (rank << top), row.shape).T
    ordered = jnp.sum(
        jnp.where((both >> top) == lane, both & ((1 << top) - 1), 0), axis=0, keepdims=True
    )
    sorted_ref[...] = ordered
    ordered_owner = (ordered >> owner_at) & (2 * columns - 1)
    group = one_lane & (groups - 1)
    coded = ordered + ((group + 1) << top)

    def lookup(mask):
        found = jnp.sum(jnp.where(mask, coded, 0), axis=1, keepdims=True)
        live = jnp.where(found > 0, 1, 0)
        source = jnp.maximum((found >> top) - 1, 0)
        return live, source, (found >> layer_at) & (LAYERS - 1), (found >> owner_at) & 1

    live, _, my_layer, core = lookup(((ordered_owner >> 1) == me_column) & (group == me_x))
    place = [live, core, my_layer]
    for s in range(OCAP):
        mask = (ordered_owner == me_column * 2 + me_c) & ((ordered >> slot_at) == s)
        place += list(lookup(mask)[:3])
    wide = lax.broadcasted_iota(i32, place_ref.shape, 1)
    out = jnp.zeros(place_ref.shape, i32)
    for number, value in enumerate(place):
        out = jnp.where(wide == number, value, out)
    place_ref[...] = out


def pack_stats_body(
    owner_ref, count_ref, stats_ref, out_ref, sorted_ref, place_ref, stats_vmem, order_ref, sems, *, groups, columns
):
    blocks = owner_ref.shape[1]
    pairs_each = out_ref.shape[1]
    load = pltpu.make_async_copy(stats_ref, stats_vmem, sems.at[0])
    load.start()
    index_body(owner_ref, count_ref, sorted_ref, place_ref, groups=groups, columns=columns)
    move = pltpu.make_async_copy(sorted_ref, order_ref, sems.at[1])
    move.start()
    move.wait()
    load.wait()
    row_block = lax.axis_index(("z", "y")) * 8 // out_ref.shape[3]
    paired = pl.ds(pl.multiple_of(8 * (row_block >> 1), 8), 8)
    single = pl.ds(pl.multiple_of(8 * (1 - (row_block >> 1)), 8), 8)
    lower = ((row_block + 1) & 2) == 0
    for x in range(groups):

        def step(i, carry, x=x):
            places = []
            for k in range(2):
                info = order_ref[0, (2 * i + k) * groups + x]
                places.append((2 * (info & (blocks - 1)), (info >> bits(blocks)) & 1))
            for c in range(2):
                slabs = [block + (core ^ c) for block, core in places]
                pairs = [stats_vmem[slab, paired, :] for slab in slabs]
                even, odd = joined(*[stats_vmem[slab, single, :] for slab in slabs])
                out_ref[x * 2 + c, i, 0:16] = jnp.concatenate(pairs, axis=0).astype(bf16)
                out_ref[x * 2 + c, i, 16:24] = jnp.where(lower, odd, even).astype(bf16)
            return carry

        lax.fori_loop(0, pairs_each, step, 0, unroll=4 if pairs_each % 4 == 0 else 1)


def grad_half_body(order_ref, grad_ref, out_ref, *, groups, blocks):
    me = lax.axis_index("dp")
    at = 8 * (1 - lax.axis_index("c"))

    def step(k, carry):
        block = order_ref[0, k * groups + me] & (blocks - 1)
        out_ref[k] = grad_ref[block, pl.ds(pl.multiple_of(at, 8), 8), :]
        return carry

    each = blocks // groups
    lax.fori_loop(0, each, step, 0, unroll=8 if each % 8 == 0 else 1)


def sum_stats_body(order_ref, got_ref, grad_ref, theirs_ref, out_ref, *, groups, blocks):
    out_ref[...] = jnp.zeros(out_ref.shape, bf16)
    me = lax.axis_index("dp")
    core = lax.axis_index("c")
    half = pl.ds(pl.multiple_of(8 * core, 8), 8)

    def step(i, carry):
        sums = []
        for c in range(2):
            total = got_ref[c, i].astype(f32)
            for x in range(1, groups):
                total = total + got_ref[2 * x + c, i].astype(f32)
            sums.append(total)
        joints = [joined(sums[0][8 * v : 8 * v + 8], sums[1][8 * v : 8 * v + 8]) for v in range(3)]
        for k in range(2):
            info = order_ref[0, (2 * i + k) * groups + me]
            column = (info >> (bits(blocks) + 1)) & (out_ref.shape[0] - 1)
            mine = grad_ref[info & (blocks - 1), half, :].astype(f32)
            theirs = theirs_ref[2 * i + k].astype(f32)
            grad = joined(jnp.where(core == 0, mine, theirs), jnp.where(core == 0, theirs, mine))
            out_ref[column, 0:16] = jnp.concatenate(joints[k], axis=0).astype(bf16)
            rest = jnp.concatenate([joints[2][k], grad[0]], axis=0)
            out_ref[column, 16:32] = rest.astype(bf16)
            out_ref[column, 32:40] = grad[1].astype(bf16)
        return carry

    pairs = got_ref.shape[1]
    lax.fori_loop(0, pairs, step, 0, unroll=2 if pairs % 2 == 0 else 1)


def dot(a, b):
    return jnp.dot(a, b, preferred_element_type=f32)


def newton_body(got_ref, out_ref, a_ref):
    order = out_ref.shape[1]
    chunk = got_ref.shape[2]
    each = chunk // 8
    for row in range(4):
        rows = slice(row * chunk, (row + 1) * chunk)
        for number, q in enumerate((row // 2 * 2, row // 2 * 2 + 1, SINGLE[row])):
            tile = got_ref[row * each : (row + 1) * each, 8 * number : 8 * number + 8, :]
            tile = tile.astype(f32).reshape(chunk, chunk)
            a_ref[rows, q * chunk : (q + 1) * chunk] = tile
            if MISSING[q] == row:
                a_ref[q * chunk : (q + 1) * chunk, rows] = tile.T
    for q in range(2):
        tile = got_ref[:, 24 + 8 * q : 32 + 8 * q, :].astype(f32).reshape(order, chunk).astype(bf16)
        for v in range(2):
            place = slice((2 * v + q) * chunk, (2 * v + q + 1) * chunk)
            out_ref[order:, place] = tile[v * order // 2 : (v + 1) * order // 2]
    a = a_ref[...]
    mean = jnp.sum(a * a, keepdims=True) * (1.0 / (order * order))
    magnitude = order * jnp.sqrt(mean + 1e-06)
    n = a * (0.25 / magnitude)
    nb = n.astype(bf16)
    e = dot(nb, nb) - 2.5 * n
    eb = e.astype(bf16)
    h = dot(eb, eb) + 3.125 * e
    n1 = dot(h.astype(bf16), nb) + 2.44140625 * n
    n1b = n1.astype(bf16)
    d = dot(nb, n1b) - 1.25 * (n + n1)
    e1 = dot(n1b, n1b) - 2.5 * n1
    e1b = e1.astype(bf16)
    h1 = dot(e1b, e1b) + 3.125 * e1
    n2 = dot(h1.astype(bf16), n1b) + 2.44140625 * n1
    x = 1.25 * d - 1.5625 * n2 - dot(d.astype(bf16), n2.astype(bf16))
    diagonal = lax.broadcasted_iota(i32, x.shape, 0) == lax.broadcasted_iota(i32, x.shape, 1)
    x = x + jnp.where(diagonal, 1.953125, 0.0)
    out_ref[0:order] = (x * (1.0 / jnp.sqrt(jnp.sqrt(magnitude)))).astype(bf16)


def raw_body(place_ref, mine_ref, other_ref, *refs):
    norm_ref, both_ref, raw_ref, sems = refs[-4:]
    out_refs = refs[:-4]
    groups = len(out_refs)
    order = mine_ref.shape[1]
    half, quarter = order // 2, order // groups
    live, core, layer = place_ref[0, 0], place_ref[0, 1], place_ref[0, 2]
    me_c, me_x = lax.axis_index("c"), lax.axis_index("dp")
    loads = [
        pltpu.make_async_copy(mine_ref, both_ref.at[me_c], sems.at[0]),
        pltpu.make_async_copy(other_ref, both_ref.at[1 - me_c], sems.at[1]),
    ]
    for load in loads:
        load.start()
    for load in loads:
        load.wait()
    raw = jnp.zeros((order, order), f32)
    grad_sq = jnp.zeros((1, 1), f32)
    for c in range(2):
        middle = jnp.zeros((order, half), f32)
        for v in range(2):
            grad = both_ref[c, order:, v * half : (v + 1) * half]
            middle = middle + dot(both_ref[core, 0:order, v * half : (v + 1) * half], grad)
            wide = grad.astype(f32)
            grad_sq = grad_sq + jnp.sum(wide * wide, keepdims=True)
        raw = raw + dot(middle.astype(bf16), both_ref[1 - core, c * half : (c + 1) * half])
    raw_sq = jnp.sum(raw * raw, keepdims=True)
    lane = lax.broadcasted_iota(i32, (1, LANES), 1)
    norms = jnp.where(lane == layer, grad_sq, 0.0) + jnp.where(lane == layer + LAYERS, raw_sq, 0.0)
    norms = jnp.where(live > 0, norms, 0.0)
    norm_ref[...] = jnp.broadcast_to(norms[:, None, :], norm_ref.shape)
    raw_ref[...] = raw.astype(bf16)
    for number, out_ref in enumerate(out_refs):
        start = ((me_x + number) & (groups - 1)) * quarter
        out_ref[...] = raw_ref[pl.ds(pl.multiple_of(start, quarter), quarter), :]


def scale_body(place_ref, norm_ref, raw_ref, *refs):
    out_ref = refs[-1]
    groups = len(refs)
    total = jnp.sum(norm_ref[...], axis=0)
    lane = lax.broadcasted_iota(i32, (1, LANES), 1)
    me_x = lax.axis_index("dp")
    for s in range(OCAP):
        live, source, layer = place_ref[0, 3 + 3 * s], place_ref[0, 4 + 3 * s], place_ref[0, 5 + 3 * s]
        grad_total = jnp.sum(jnp.where(lane == layer, total, 0.0), keepdims=True)
        raw_total = jnp.sum(jnp.where(lane == layer + LAYERS, total, 0.0), keepdims=True)
        ratio = jnp.sqrt((grad_total + 1e-06) / (raw_total + 1e-06))
        ratio = jnp.where(live > 0, ratio, 0.0)
        step = jnp.where(live > 0, (me_x - source) & (groups - 1), groups)
        for number in range(groups):

            @pl.when(step == number)
            def _(number=number, s=s, ratio=ratio):
                block = raw_ref[...] if number == 0 else refs[number - 1][...]
                out_ref[s] = (block.astype(f32) * ratio).astype(bf16)

        @pl.when(step == groups)
        def _(s=s):
            out_ref[s] = jnp.zeros(out_ref.shape[1:], bf16)


def on_device(stats_partial, gradient, owner_of, layer_count):
    groups = lax.axis_size("dp")
    columns = lax.axis_size("z") * lax.axis_size("y")
    blocks = owner_of.shape[0]
    each = blocks // groups
    local_rows, order = gradient.shape[1:]
    quarter = order // groups
    chunk = order // 4
    struct = jax.ShapeDtypeStruct
    swap = [(0, 1), (1, 0)]

    stats = packed(stats_partial.reshape(2 * blocks, local_rows, order))
    out_shape = (2 * groups, each // 2, 24, chunk)
    outgoing, order_info, place = call(
        functools.partial(pack_stats_body, groups=groups, columns=columns),
        (pltpu.VMEM(out_shape, bf16), struct((1, blocks), i32), struct((1, 128), i32)),
        [VMEM, SMEM, ANY],
        [
            pltpu.VMEM(stats.shape, f32),
            pltpu.SMEM((1, blocks), i32),
            pltpu.SemaphoreType.DMA((2,)),
        ],
        (VMEM, VMEM, VMEM),
    )(in_hbm(owner_of[None]), in_hbm(layer_count), in_hbm(stats))
    arrived = lax.all_to_all(outgoing, ("dp", "c"), 0, 0, tiled=True)
    grad = packed(gradient)
    grad_half = call(
        functools.partial(grad_half_body, groups=groups, blocks=blocks),
        pltpu.VMEM((each, 8, chunk), bf16),
        [SMEM, VMEM],
    )(order_info, grad)
    grad_theirs = lax.ppermute(grad_half, "c", swap)
    summed = call(
        functools.partial(sum_stats_body, groups=groups, blocks=blocks),
        pltpu.VMEM((columns, 40, chunk), bf16),
        [SMEM, VMEM, VMEM, VMEM],
    )(order_info, held(arrived), grad, held(grad_theirs))
    statistic = lax.all_to_all(summed, ("z", "y"), 0, 0, tiled=True)
    bundle_shape = (order + order // 2, order)
    bundle = call(
        newton_body, pltpu.VMEM(bundle_shape, bf16), [VMEM], [pltpu.VMEM((order, order), f32)]
    )(held(statistic))
    other = lax.ppermute(bundle, "c", swap)
    *quarters, norms = call(
        raw_body,
        tuple(pltpu.VMEM((quarter, order), bf16) for _ in range(groups))
        + (pltpu.VMEM((groups * columns, 1, LANES), f32),),
        [SMEM, ANY, ANY],
        [
            pltpu.VMEM((2, *bundle_shape), bf16),
            pltpu.VMEM((order, order), bf16),
            pltpu.SemaphoreType.DMA((2,)),
        ],
        (VMEM,) * (groups + 1),
    )(place, held(bundle), held(other))
    norms = lax.all_to_all(norms, ("dp", "z", "y"), 0, 0, tiled=True)
    spread = [held(quarters[0])]
    for step in range(1, groups):
        pairs = [(i, (i + step) % groups) for i in range(groups)]
        spread.append(held(lax.ppermute(quarters[step], "dp", pairs)))
    out = call(
        scale_body, struct((OCAP, quarter, order), bf16), [SMEM] + [VMEM] * (groups + 1)
    )(place, held(norms), *spread)
    return out[None]


def solution(mesh):
    shards = mesh.shape["shard"]
    side = 1
    while (2 * side) ** 2 * 2 <= shards:
        side *= 2
    torus = Mesh(
        mesh.devices.reshape(mesh.shape["dp"], shards // (2 * side), side, 2), ("dp", "z", "y", "c")
    )
    placed = (P("dp", None, None, SHARD, None), P(None, SHARD, None), P(), P())
    return jax.shard_map(
        on_device,
        mesh=torus,
        in_specs=placed,
        out_specs=P(SHARD, None, "dp", None),
        check_vma=False,
    )
```

```python
import functools

import jax
import jax.numpy as jnp
from jax import lax
from jax.experimental import pallas as pl
from jax.experimental.pallas import tpu as pltpu
from jax.sharding import Mesh
from jax.sharding import PartitionSpec as P

OCAP = 2
LAYERS = 4
LANES = 128
SHARD = ("z", "y", "c")
bf16, f32, i32 = jnp.bfloat16, jnp.float32, jnp.int32
SMEM = pl.BlockSpec(memory_space=pltpu.SMEM)
VMEM = pl.BlockSpec(memory_space=pltpu.VMEM)


ANY = pl.BlockSpec(memory_space=pl.ANY)


def bits(size):
    assert size & (size - 1) == 0
    return size.bit_length() - 1


def held(x):
    return pltpu.with_memory_space_constraint(x, pltpu.VMEM)


def in_smem(x):
    return pltpu.with_memory_space_constraint(x, pltpu.SMEM)


def in_hbm(x):
    return pltpu.with_memory_space_constraint(x, pltpu.HBM)


def call(body, out_shape, in_specs, scratch=(), out_specs=None):
    return pl.pallas_call(
        body,
        out_shape=out_shape,
        in_specs=in_specs,
        out_specs=VMEM if out_specs is None else out_specs,
        scratch_shapes=list(scratch),
        compiler_params=pltpu.CompilerParams(vmem_limit_bytes=24 * 2**20),
    )


def packed(x):
    n, r, width = x.shape
    return x.reshape(n, r, 4, width // 4).transpose(0, 2, 1, 3).reshape(n, 4 * r, width // 4)


SINGLE = (3, 2, 0, 1)
MISSING = (2, 3, 1, 0)


def joined(first, second):
    top = lax.broadcasted_iota(i32, first.shape, 0) < 4
    even = jnp.where(top, first, pltpu.roll(second, 4, 0))
    odd = jnp.where(top, pltpu.roll(first, 4, 0), second)
    return even, odd


def index_body(owner_ref, count_ref, sorted_ref, place_ref, *, groups, columns):
    blocks = owner_ref.shape[1]
    me_x, me_c, me_column = lax.axis_index("dp"), lax.axis_index("c"), lax.axis_index(("z", "y"))
    owner = owner_ref[...]
    row = jnp.broadcast_to(owner, (blocks, blocks))
    col = row.T
    sub = lax.broadcasted_iota(i32, row.shape, 0)
    lane = lax.broadcasted_iota(i32, row.shape, 1)
    same = (col == row) & (sub < lane)
    rank = jnp.sum(jnp.where((col < row) | same, 1, 0), axis=0, keepdims=True)
    slot = jnp.sum(jnp.where(same, 1, 0), axis=0, keepdims=True)
    one_lane = lax.broadcasted_iota(i32, owner.shape, 1)
    layer = jnp.zeros(owner.shape, i32)
    end = jnp.int32(0)
    for number in range(LAYERS - 1):
        end = end + count_ref[number]
        layer = layer + jnp.where(one_lane >= end, 1, 0)
    owner_at = bits(blocks)
    layer_at = owner_at + bits(2 * columns)
    slot_at = layer_at + bits(LAYERS)
    top = slot_at + bits(OCAP)
    info = one_lane + (owner << owner_at) + (layer << layer_at) + (slot << slot_at)
    both = jnp.broadcast_to(info + (rank << top), row.shape).T
    ordered = jnp.sum(
        jnp.where((both >> top) == lane, both & ((1 << top) - 1), 0), axis=0, keepdims=True
    )
    sorted_ref[...] = ordered
    ordered_owner = (ordered >> owner_at) & (2 * columns - 1)
    group = one_lane & (groups - 1)
    coded = ordered + ((group + 1) << top)

    def lookup(mask):
        found = jnp.sum(jnp.where(mask, coded, 0), axis=1, keepdims=True)
        live = jnp.where(found > 0, 1, 0)
        source = jnp.maximum((found >> top) - 1, 0)
        return live, source, (found >> layer_at) & (LAYERS - 1), (found >> owner_at) & 1

    live, _, my_layer, core = lookup(((ordered_owner >> 1) == me_column) & (group == me_x))
    place = [live, core, my_layer]
    for s in range(OCAP):
        mask = (ordered_owner == me_column * 2 + me_c) & ((ordered >> slot_at) == s)
        place += list(lookup(mask)[:3])
    wide = lax.broadcasted_iota(i32, place_ref.shape, 1)
    out = jnp.zeros(place_ref.shape, i32)
    for number, value in enumerate(place):
        out = jnp.where(wide == number, value, out)
    place_ref[...] = out


def pack_stats_body(
    owner_ref,
    count_ref,
    stats_ref,
    out_ref,
    sorted_ref,
    place_ref,
    owner_vmem,
    count_smem,
    stats_vmem,
    out_vmem,
    order_ref,
    sems,
    *,
    groups,
    columns,
):
    blocks = owner_ref.shape[1]
    pairs_each = out_ref.shape[1]
    small = [
        pltpu.make_async_copy(owner_ref, owner_vmem, sems.at[1]),
        pltpu.make_async_copy(count_ref, count_smem, sems.at[2]),
    ]
    load = pltpu.make_async_copy(stats_ref, stats_vmem, sems.at[0])
    for copy in small:
        copy.start()
    load.start()
    for copy in small:
        copy.wait()
    index_body(owner_vmem, count_smem, sorted_ref, place_ref, groups=groups, columns=columns)
    move = pltpu.make_async_copy(sorted_ref, order_ref, sems.at[3])
    move.start()
    move.wait()
    load.wait()
    stores = []
    row_block = lax.axis_index(("z", "y")) * 8 // out_ref.shape[3]
    paired = pl.ds(pl.multiple_of(8 * (row_block >> 1), 8), 8)
    single = pl.ds(pl.multiple_of(8 * (1 - (row_block >> 1)), 8), 8)
    lower = ((row_block + 1) & 2) == 0
    for x in range(groups):

        def step(i, carry, x=x):
            places = []
            for k in range(2):
                info = order_ref[0, (2 * i + k) * groups + x]
                places.append((2 * (info & (blocks - 1)), (info >> bits(blocks)) & 1))
            for c in range(2):
                slabs = [block + (core ^ c) for block, core in places]
                pairs = [stats_vmem[slab, paired, :] for slab in slabs]
                even, odd = joined(*[stats_vmem[slab, single, :] for slab in slabs])
                out_vmem[x * 2 + c, i, 0:16] = jnp.concatenate(pairs, axis=0).astype(bf16)
                out_vmem[x * 2 + c, i, 16:24] = jnp.where(lower, odd, even).astype(bf16)
            return carry

        lax.fori_loop(0, pairs_each, step, 0, unroll=4 if pairs_each % 4 == 0 else 1)
        part = pl.ds(2 * x, 2)
        stores.append(pltpu.make_async_copy(out_vmem.at[part], out_ref.at[part], sems.at[4 + x]))
        stores[-1].start()
    for store in stores:
        store.wait()


def grad_half_body(order_ref, grad_ref, out_ref, *, groups, blocks):
    me = lax.axis_index("dp")
    at = 8 * (1 - lax.axis_index("c"))

    def step(k, carry):
        block = order_ref[0, k * groups + me] & (blocks - 1)
        out_ref[k] = grad_ref[block, pl.ds(pl.multiple_of(at, 8), 8), :]
        return carry

    each = blocks // groups
    lax.fori_loop(0, each, step, 0, unroll=8 if each % 8 == 0 else 1)


def sum_stats_body(order_ref, got_ref, grad_ref, theirs_ref, out_ref, *, groups, blocks):
    out_ref[...] = jnp.zeros(out_ref.shape, bf16)
    me = lax.axis_index("dp")
    core = lax.axis_index("c")
    half = pl.ds(pl.multiple_of(8 * core, 8), 8)

    def step(i, carry):
        sums = []
        for c in range(2):
            total = got_ref[c, i].astype(f32)
            for x in range(1, groups):
                total = total + got_ref[2 * x + c, i].astype(f32)
            sums.append(total)
        joints = [joined(sums[0][8 * v : 8 * v + 8], sums[1][8 * v : 8 * v + 8]) for v in range(3)]
        for k in range(2):
            info = order_ref[0, (2 * i + k) * groups + me]
            column = (info >> (bits(blocks) + 1)) & (out_ref.shape[0] - 1)
            mine = grad_ref[info & (blocks - 1), half, :].astype(f32)
            theirs = theirs_ref[2 * i + k].astype(f32)
            grad = joined(jnp.where(core == 0, mine, theirs), jnp.where(core == 0, theirs, mine))
            out_ref[column, 0:16] = jnp.concatenate(joints[k], axis=0).astype(bf16)
            rest = jnp.concatenate([joints[2][k], grad[0]], axis=0)
            out_ref[column, 16:32] = rest.astype(bf16)
            out_ref[column, 32:40] = grad[1].astype(bf16)
        return carry

    pairs = got_ref.shape[1]
    lax.fori_loop(0, pairs, step, 0, unroll=2 if pairs % 2 == 0 else 1)


def dot(a, b):
    return jnp.dot(a, b, preferred_element_type=f32)


def newton_body(got_ref, out_ref, a_ref):
    order = out_ref.shape[1]
    chunk = got_ref.shape[2]
    each = chunk // 8
    for row in range(4):
        rows = slice(row * chunk, (row + 1) * chunk)
        for number, q in enumerate((row // 2 * 2, row // 2 * 2 + 1, SINGLE[row])):
            tile = got_ref[row * each : (row + 1) * each, 8 * number : 8 * number + 8, :]
            tile = tile.astype(f32).reshape(chunk, chunk)
            a_ref[rows, q * chunk : (q + 1) * chunk] = tile
            if MISSING[q] == row:
                a_ref[q * chunk : (q + 1) * chunk, rows] = tile.T
    for q in range(2):
        tile = got_ref[:, 24 + 8 * q : 32 + 8 * q, :].astype(f32).reshape(order, chunk).astype(bf16)
        for v in range(2):
            place = slice((2 * v + q) * chunk, (2 * v + q + 1) * chunk)
            out_ref[order:, place] = tile[v * order // 2 : (v + 1) * order // 2]
    a = a_ref[...]
    mean = jnp.sum(a * a, keepdims=True) * (1.0 / (order * order))
    magnitude = order * jnp.sqrt(mean + 1e-06)
    n = a * (0.25 / magnitude)
    nb = n.astype(bf16)
    e = dot(nb, nb) - 2.5 * n
    eb = e.astype(bf16)
    h = dot(eb, eb) + 3.125 * e
    n1 = dot(h.astype(bf16), nb) + 2.44140625 * n
    n1b = n1.astype(bf16)
    d = dot(nb, n1b) - 1.25 * (n + n1)
    e1 = dot(n1b, n1b) - 2.5 * n1
    e1b = e1.astype(bf16)
    h1 = dot(e1b, e1b) + 3.125 * e1
    n2 = dot(h1.astype(bf16), n1b) + 2.44140625 * n1
    x = 1.25 * d - 1.5625 * n2 - dot(d.astype(bf16), n2.astype(bf16))
    diagonal = lax.broadcasted_iota(i32, x.shape, 0) == lax.broadcasted_iota(i32, x.shape, 1)
    x = x + jnp.where(diagonal, 1.953125, 0.0)
    out_ref[0:order] = (x * (1.0 / jnp.sqrt(jnp.sqrt(magnitude)))).astype(bf16)


def raw_body(place_ref, mine_ref, other_ref, *refs):
    norm_ref, raw_ref = refs[-2:]
    out_refs = refs[:-2]
    groups = len(out_refs)
    order = mine_ref.shape[1]
    half, quarter = order // 2, order // groups
    live, core, layer = place_ref[0, 0], place_ref[0, 1], place_ref[0, 2]
    me_c, me_x = lax.axis_index("c"), lax.axis_index("dp")
    grad_sq = jnp.zeros((1, 1), f32)
    for ref in (mine_ref, other_ref):
        wide = ref[order:].astype(f32)
        grad_sq = grad_sq + jnp.sum(wide * wide, keepdims=True)
    lane = lax.broadcasted_iota(i32, (1, LANES), 1)

    def finish(left_ref, right_ref):
        raw = jnp.zeros((order, order), f32)
        for ref, at in ((mine_ref, me_c), (other_ref, 1 - me_c)):
            middle = jnp.zeros((order, half), f32)
            for v in range(2):
                cols = slice(v * half, (v + 1) * half)
                middle = middle + dot(left_ref[0:order, cols], ref[order:, cols])
            right = right_ref[pl.ds(pl.multiple_of(at * half, half), half), :]
            raw = raw + dot(middle.astype(bf16), right)
        raw_sq = jnp.sum(raw * raw, keepdims=True)
        norms = jnp.where(lane == layer, grad_sq, 0.0)
        norms = norms + jnp.where(lane == layer + LAYERS, raw_sq, 0.0)
        norms = jnp.where(live > 0, norms, 0.0)
        norm_ref[...] = jnp.broadcast_to(norms[:, None, :], norm_ref.shape)
        raw_ref[...] = raw.astype(bf16)

    @pl.when(core == me_c)
    def _():
        finish(mine_ref, other_ref)

    @pl.when(core != me_c)
    def _():
        finish(other_ref, mine_ref)

    for number, out_ref in enumerate(out_refs):
        start = ((me_x + number) & (groups - 1)) * quarter
        out_ref[...] = raw_ref[pl.ds(pl.multiple_of(start, quarter), quarter), :]


def scale_body(place_ref, norm_ref, raw_ref, *refs):
    out_ref = refs[-1]
    groups = len(refs)
    total = jnp.sum(norm_ref[...], axis=0)
    lane = lax.broadcasted_iota(i32, (1, LANES), 1)
    me_x = lax.axis_index("dp")
    for s in range(OCAP):
        live, source, layer = place_ref[0, 3 + 3 * s], place_ref[0, 4 + 3 * s], place_ref[0, 5 + 3 * s]
        grad_total = jnp.sum(jnp.where(lane == layer, total, 0.0), keepdims=True)
        raw_total = jnp.sum(jnp.where(lane == layer + LAYERS, total, 0.0), keepdims=True)
        ratio = jnp.sqrt((grad_total + 1e-06) / (raw_total + 1e-06))
        ratio = jnp.where(live > 0, ratio, 0.0)
        step = jnp.where(live > 0, (me_x - source) & (groups - 1), groups)
        for number in range(groups):

            @pl.when(step == number)
            def _(number=number, s=s, ratio=ratio):
                block = raw_ref[...] if number == 0 else refs[number - 1][...]
                out_ref[s] = (block.astype(f32) * ratio).astype(bf16)

        @pl.when(step == groups)
        def _(s=s):
            out_ref[s] = jnp.zeros(out_ref.shape[1:], bf16)


def on_device(stats_partial, gradient, owner_of, layer_count):
    groups = lax.axis_size("dp")
    columns = lax.axis_size("z") * lax.axis_size("y")
    blocks = owner_of.shape[0]
    each = blocks // groups
    local_rows, order = gradient.shape[1:]
    quarter = order // groups
    chunk = order // 4
    struct = jax.ShapeDtypeStruct
    swap = [(0, 1), (1, 0)]

    stats = packed(stats_partial.reshape(2 * blocks, local_rows, order))
    out_shape = (2 * groups, each // 2, 24, chunk)
    outgoing, order_info, place = call(
        functools.partial(pack_stats_body, groups=groups, columns=columns),
        (struct(out_shape, bf16), struct((1, blocks), i32), struct((1, 128), i32)),
        [ANY, ANY, ANY],
        [
            pltpu.VMEM((1, blocks), i32),
            pltpu.SMEM((LAYERS,), i32),
            pltpu.VMEM(stats.shape, f32),
            pltpu.VMEM(out_shape, bf16),
            pltpu.SMEM((1, blocks), i32),
            pltpu.SemaphoreType.DMA((4 + groups,)),
        ],
        (ANY, VMEM, VMEM),
    )(in_hbm(owner_of[None]), in_hbm(layer_count), in_hbm(stats))
    order_info, place = in_smem(order_info), in_smem(place)
    arrived = lax.all_to_all(outgoing, ("dp", "c"), 0, 0, tiled=True)
    grad = packed(gradient)
    grad_half = call(
        functools.partial(grad_half_body, groups=groups, blocks=blocks),
        pltpu.VMEM((each, 8, chunk), bf16),
        [SMEM, VMEM],
    )(order_info, grad)
    grad_theirs = lax.ppermute(grad_half, "c", swap)
    summed = call(
        functools.partial(sum_stats_body, groups=groups, blocks=blocks),
        pltpu.VMEM((columns, 40, chunk), bf16),
        [SMEM, VMEM, VMEM, VMEM],
    )(order_info, held(arrived), grad, held(grad_theirs))
    statistic = lax.all_to_all(summed, ("z", "y"), 0, 0, tiled=True)
    bundle_shape = (order + order // 2, order)
    bundle = call(
        newton_body, pltpu.VMEM(bundle_shape, bf16), [VMEM], [pltpu.VMEM((order, order), f32)]
    )(held(statistic))
    other = lax.ppermute(bundle, "c", swap)
    *quarters, norms = call(
        raw_body,
        tuple(pltpu.VMEM((quarter, order), bf16) for _ in range(groups))
        + (pltpu.VMEM((groups * columns, 1, LANES), f32),),
        [SMEM, VMEM, VMEM],
        [pltpu.VMEM((order, order), bf16)],
        (VMEM,) * (groups + 1),
    )(place, held(bundle), held(other))
    norms = lax.all_to_all(norms, ("dp", "z", "y"), 0, 0, tiled=True)
    spread = [held(quarters[0])]
    for step in range(1, groups):
        pairs = [(i, (i + step) % groups) for i in range(groups)]
        spread.append(held(lax.ppermute(quarters[step], "dp", pairs)))
    out = call(
        scale_body, struct((OCAP, quarter, order), bf16), [SMEM] + [VMEM] * (groups + 1)
    )(place, held(norms), *spread)
    return out[None]


def solution(mesh):
    shards = mesh.shape["shard"]
    side = 1
    while (2 * side) ** 2 * 2 <= shards:
        side *= 2
    torus = Mesh(
        mesh.devices.reshape(mesh.shape["dp"], shards // (2 * side), side, 2), ("dp", "z", "y", "c")
    )
    placed = (P("dp", None, None, SHARD, None), P(None, SHARD, None), P(), P())
    return jax.shard_map(
        on_device,
        mesh=torus,
        in_specs=placed,
        out_specs=P(SHARD, None, "dp", None),
        check_vma=False,
    )
```

```python
import functools

import jax
import jax.numpy as jnp
from jax import lax
from jax.experimental import pallas as pl
from jax.experimental.pallas import tpu as pltpu
from jax.sharding import Mesh
from jax.sharding import PartitionSpec as P

OCAP = 2
LAYERS = 4
LANES = 128
SHARD = ("z", "y", "c")
bf16, f32, i32 = jnp.bfloat16, jnp.float32, jnp.int32
SMEM = pl.BlockSpec(memory_space=pltpu.SMEM)
VMEM = pl.BlockSpec(memory_space=pltpu.VMEM)


ANY = pl.BlockSpec(memory_space=pl.ANY)


def bits(size):
    assert size & (size - 1) == 0
    return size.bit_length() - 1


def held(x):
    return pltpu.with_memory_space_constraint(x, pltpu.VMEM)


def in_hbm(x):
    return pltpu.with_memory_space_constraint(x, pltpu.HBM)


def call(body, out_shape, in_specs, scratch=(), out_specs=None):
    return pl.pallas_call(
        body,
        out_shape=out_shape,
        in_specs=in_specs,
        out_specs=VMEM if out_specs is None else out_specs,
        scratch_shapes=list(scratch),
        compiler_params=pltpu.CompilerParams(vmem_limit_bytes=24 * 2**20),
    )


def square_sum(x):
    rows, width = x.shape
    return jnp.sum(jnp.sum((x * x).reshape(rows // 8, 8, width), axis=0), keepdims=True)


def packed(x):
    n, r, width = x.shape
    return x.reshape(n, r, 4, width // 4).transpose(0, 2, 1, 3).reshape(n, 4 * r, width // 4)


SINGLE = (3, 2, 0, 1)
MISSING = (2, 3, 1, 0)


def joined(first, second):
    top = lax.broadcasted_iota(i32, first.shape, 0) < 4
    even = jnp.where(top, first, pltpu.roll(second, 4, 0))
    odd = jnp.where(top, pltpu.roll(first, 4, 0), second)
    return even, odd


def index_body(owner_ref, count_ref, sorted_ref, place_ref, *, groups, columns):
    blocks = owner_ref.shape[1]
    me_x, me_c, me_column = lax.axis_index("dp"), lax.axis_index("c"), lax.axis_index(("z", "y"))
    owner = owner_ref[...]
    row = jnp.broadcast_to(owner, (blocks, blocks))
    col = row.T
    sub = lax.broadcasted_iota(i32, row.shape, 0)
    lane = lax.broadcasted_iota(i32, row.shape, 1)
    same = (col == row) & (sub < lane)
    rank = jnp.sum(jnp.where((col < row) | same, 1, 0), axis=0, keepdims=True)
    slot = jnp.sum(jnp.where(same, 1, 0), axis=0, keepdims=True)
    one_lane = lax.broadcasted_iota(i32, owner.shape, 1)
    layer = jnp.zeros(owner.shape, i32)
    end = jnp.int32(0)
    for number in range(LAYERS - 1):
        end = end + count_ref[number]
        layer = layer + jnp.where(one_lane >= end, 1, 0)
    owner_at = bits(blocks)
    layer_at = owner_at + bits(2 * columns)
    slot_at = layer_at + bits(LAYERS)
    top = slot_at + bits(OCAP)
    info = one_lane + (owner << owner_at) + (layer << layer_at) + (slot << slot_at)
    both = jnp.broadcast_to(info + (rank << top), row.shape).T
    ordered = jnp.sum(
        jnp.where((both >> top) == lane, both & ((1 << top) - 1), 0), axis=0, keepdims=True
    )
    sorted_ref[...] = ordered
    ordered_owner = (ordered >> owner_at) & (2 * columns - 1)
    group = one_lane & (groups - 1)
    coded = ordered + ((group + 1) << top)

    def lookup(mask):
        found = jnp.sum(jnp.where(mask, coded, 0), axis=1, keepdims=True)
        live = jnp.where(found > 0, 1, 0)
        source = jnp.maximum((found >> top) - 1, 0)
        return live, source, (found >> layer_at) & (LAYERS - 1), (found >> owner_at) & 1

    live, _, my_layer, core = lookup(((ordered_owner >> 1) == me_column) & (group == me_x))
    place = [live, core, my_layer]
    for s in range(OCAP):
        mask = (ordered_owner == me_column * 2 + me_c) & ((ordered >> slot_at) == s)
        place += list(lookup(mask)[:3])
    wide = lax.broadcasted_iota(i32, place_ref.shape, 1)
    out = jnp.zeros(place_ref.shape, i32)
    for number, value in enumerate(place):
        out = jnp.where(wide == number, value, out)
    place_ref[...] = out


def pack_stats_body(
    owner_ref,
    count_ref,
    stats_ref,
    out_ref,
    sorted_ref,
    place_ref,
    owner_vmem,
    count_smem,
    stats_vmem,
    out_vmem,
    order_ref,
    sems,
    *,
    groups,
    columns,
):
    blocks = owner_ref.shape[1]
    pairs_each = out_ref.shape[1]
    small = [
        pltpu.make_async_copy(owner_ref, owner_vmem, sems.at[1]),
        pltpu.make_async_copy(count_ref, count_smem, sems.at[2]),
    ]
    load = pltpu.make_async_copy(stats_ref, stats_vmem, sems.at[0])
    for copy in small:
        copy.start()
    load.start()
    for copy in small:
        copy.wait()
    index_body(owner_vmem, count_smem, sorted_ref, place_ref, groups=groups, columns=columns)
    move = pltpu.make_async_copy(sorted_ref, order_ref, sems.at[3])
    move.start()
    move.wait()
    load.wait()
    stores = []
    row_block = lax.axis_index(("z", "y")) * 8 // out_ref.shape[3]
    paired = pl.ds(pl.multiple_of(8 * (row_block >> 1), 8), 8)
    single = pl.ds(pl.multiple_of(8 * (1 - (row_block >> 1)), 8), 8)
    lower = ((row_block + 1) & 2) == 0
    for x in range(groups):

        def step(i, carry, x=x):
            places = []
            for k in range(2):
                info = order_ref[0, (2 * i + k) * groups + x]
                places.append((2 * (info & (blocks - 1)), (info >> bits(blocks)) & 1))
            for c in range(2):
                slabs = [block + (core ^ c) for block, core in places]
                pairs = [stats_vmem[slab, paired, :] for slab in slabs]
                even, odd = joined(*[stats_vmem[slab, single, :] for slab in slabs])
                out_vmem[x * 2 + c, i, 0:16] = jnp.concatenate(pairs, axis=0).astype(bf16)
                out_vmem[x * 2 + c, i, 16:24] = jnp.where(lower, odd, even).astype(bf16)
            return carry

        lax.fori_loop(0, pairs_each, step, 0, unroll=4 if pairs_each % 4 == 0 else 1)
        part = pl.ds(2 * x, 2)
        stores.append(pltpu.make_async_copy(out_vmem.at[part], out_ref.at[part], sems.at[4 + x]))
        stores[-1].start()
    for store in stores:
        store.wait()


def grad_half_body(order_ref, grad_ref, out_ref, *, groups, blocks):
    me = lax.axis_index("dp")
    at = 8 * (1 - lax.axis_index("c"))

    def step(k, carry):
        block = order_ref[0, k * groups + me] & (blocks - 1)
        out_ref[k] = grad_ref[block, pl.ds(pl.multiple_of(at, 8), 8), :]
        return carry

    each = blocks // groups
    lax.fori_loop(0, each, step, 0, unroll=8 if each % 8 == 0 else 1)


def sum_stats_body(info_ref, got_ref, grad_ref, theirs_ref, out_ref, order_ref, sem, *, groups, blocks):
    move = pltpu.make_async_copy(info_ref, order_ref, sem)
    move.start()
    out_ref[...] = jnp.zeros(out_ref.shape, bf16)
    move.wait()
    me = lax.axis_index("dp")
    core = lax.axis_index("c")
    half = pl.ds(pl.multiple_of(8 * core, 8), 8)

    def step(i, carry):
        sums = []
        for c in range(2):
            total = got_ref[c, i].astype(f32)
            for x in range(1, groups):
                total = total + got_ref[2 * x + c, i].astype(f32)
            sums.append(total)
        joints = [joined(sums[0][8 * v : 8 * v + 8], sums[1][8 * v : 8 * v + 8]) for v in range(3)]
        for k in range(2):
            info = order_ref[0, (2 * i + k) * groups + me]
            column = (info >> (bits(blocks) + 1)) & (out_ref.shape[0] - 1)
            mine = grad_ref[info & (blocks - 1), half, :].astype(f32)
            theirs = theirs_ref[2 * i + k].astype(f32)
            grad = joined(jnp.where(core == 0, mine, theirs), jnp.where(core == 0, theirs, mine))
            out_ref[column, 0:16] = jnp.concatenate(joints[k], axis=0).astype(bf16)
            rest = jnp.concatenate([joints[2][k], grad[0]], axis=0)
            out_ref[column, 16:32] = rest.astype(bf16)
            out_ref[column, 32:40] = grad[1].astype(bf16)
        return carry

    pairs = got_ref.shape[1]
    lax.fori_loop(0, pairs, step, 0, unroll=2 if pairs % 2 == 0 else 1)


def dot(a, b):
    return jnp.dot(a, b, preferred_element_type=f32)


def newton_body(got_ref, out_ref, a_ref):
    order = out_ref.shape[1]
    chunk = got_ref.shape[2]
    each = chunk // 8
    for row in range(4):
        rows = slice(row * chunk, (row + 1) * chunk)
        for number, q in enumerate((row // 2 * 2, row // 2 * 2 + 1, SINGLE[row])):
            tile = got_ref[row * each : (row + 1) * each, 8 * number : 8 * number + 8, :]
            tile = tile.astype(f32).reshape(chunk, chunk)
            a_ref[rows, q * chunk : (q + 1) * chunk] = tile
            if MISSING[q] == row:
                a_ref[q * chunk : (q + 1) * chunk, rows] = tile.T
    for q in range(2):
        tile = got_ref[:, 24 + 8 * q : 32 + 8 * q, :].astype(f32).reshape(order, chunk).astype(bf16)
        for v in range(2):
            place = slice((2 * v + q) * chunk, (2 * v + q + 1) * chunk)
            out_ref[order:, place] = tile[v * order // 2 : (v + 1) * order // 2]
    a = a_ref[...]
    mean = square_sum(a) * (1.0 / (order * order))
    magnitude = order * jnp.sqrt(mean + 1e-06)
    n = a * (0.25 / magnitude)
    nb = n.astype(bf16)
    e = dot(nb, nb) - 2.5 * n
    eb = e.astype(bf16)
    h = dot(eb, eb) + 3.125 * e
    n1 = dot(h.astype(bf16), nb) + 2.44140625 * n
    n1b = n1.astype(bf16)
    d = dot(nb, n1b) - 1.25 * (n + n1)
    e1 = dot(n1b, n1b) - 2.5 * n1
    e1b = e1.astype(bf16)
    h1 = dot(e1b, e1b) + 3.125 * e1
    n2 = dot(h1.astype(bf16), n1b) + 2.44140625 * n1
    x = 1.25 * d - 1.5625 * n2 - dot(d.astype(bf16), n2.astype(bf16))
    diagonal = lax.broadcasted_iota(i32, x.shape, 0) == lax.broadcasted_iota(i32, x.shape, 1)
    x = x + jnp.where(diagonal, 1.953125, 0.0)
    out_ref[0:order] = (x * (1.0 / jnp.sqrt(jnp.sqrt(magnitude)))).astype(bf16)


def raw_body(scalars_ref, mine_ref, other_ref, *refs):
    norm_ref, raw_ref, place_ref, sem = refs[-4:]
    out_refs = refs[:-4]
    move = pltpu.make_async_copy(scalars_ref, place_ref, sem)
    move.start()
    groups = len(out_refs)
    order = mine_ref.shape[1]
    half, quarter = order // 2, order // groups
    me_c, me_x = lax.axis_index("c"), lax.axis_index("dp")
    grad_sq = square_sum(mine_ref[order:].astype(f32)) + square_sum(other_ref[order:].astype(f32))
    move.wait()
    live, core, layer = place_ref[0, 0], place_ref[0, 1], place_ref[0, 2]
    lane = lax.broadcasted_iota(i32, (1, LANES), 1)

    def finish(left_ref, right_ref):
        raw = jnp.zeros((order, order), f32)
        for ref, at in ((mine_ref, me_c), (other_ref, 1 - me_c)):
            middle = jnp.zeros((order, half), f32)
            for v in range(2):
                cols = slice(v * half, (v + 1) * half)
                middle = middle + dot(left_ref[0:order, cols], ref[order:, cols])
            right = right_ref[pl.ds(pl.multiple_of(at * half, half), half), :]
            raw = raw + dot(middle.astype(bf16), right)
        raw_sq = square_sum(raw)
        norms = jnp.where(lane == layer, grad_sq, 0.0)
        norms = norms + jnp.where(lane == layer + LAYERS, raw_sq, 0.0)
        norms = jnp.where(live > 0, norms, 0.0)
        norm_ref[...] = jnp.broadcast_to(norms[:, None, :], norm_ref.shape)
        raw_ref[...] = raw.astype(bf16)

    @pl.when(core == me_c)
    def _():
        finish(mine_ref, other_ref)

    @pl.when(core != me_c)
    def _():
        finish(other_ref, mine_ref)

    for number, out_ref in enumerate(out_refs):
        start = ((me_x + number) & (groups - 1)) * quarter
        out_ref[...] = raw_ref[pl.ds(pl.multiple_of(start, quarter), quarter), :]


def scale_body(scalars_ref, norm_ref, raw_ref, *refs):
    out_ref, out_vmem, place_ref, sems = refs[-4:]
    others = refs[:-4]
    groups = len(others) + 1
    move = pltpu.make_async_copy(scalars_ref, place_ref, sems.at[0])
    move.start()
    chains = 8
    length = norm_ref.shape[0] // chains
    total = jnp.zeros((1, LANES), f32)
    for number in range(chains):
        total = total + jnp.sum(norm_ref[number * length : (number + 1) * length], axis=0)
    lane = lax.broadcasted_iota(i32, (1, LANES), 1)
    me_x = lax.axis_index("dp")
    move.wait()
    stores = []
    for s in range(OCAP):
        live, source, layer = place_ref[0, 3 + 3 * s], place_ref[0, 4 + 3 * s], place_ref[0, 5 + 3 * s]
        grad_total = jnp.sum(jnp.where(lane == layer, total, 0.0), keepdims=True)
        raw_total = jnp.sum(jnp.where(lane == layer + LAYERS, total, 0.0), keepdims=True)
        ratio = jnp.sqrt((grad_total + 1e-06) / (raw_total + 1e-06))
        step = jnp.where(live > 0, (me_x - source) & (groups - 1), groups)
        for number in range(groups):

            @pl.when(step == number)
            def _(number=number, s=s, ratio=ratio):
                block = raw_ref[...] if number == 0 else others[number - 1][...]
                out_vmem[s] = (block.astype(f32) * ratio).astype(bf16)

        @pl.when(step == groups)
        def _(s=s):
            out_vmem[s] = jnp.zeros(out_vmem.shape[1:], bf16)

        stores.append(pltpu.make_async_copy(out_vmem.at[s], out_ref.at[s], sems.at[1 + s]))
        stores[-1].start()
    for store in stores:
        store.wait()


def on_device(stats_partial, gradient, owner_of, layer_count):
    groups = lax.axis_size("dp")
    columns = lax.axis_size("z") * lax.axis_size("y")
    blocks = owner_of.shape[0]
    each = blocks // groups
    local_rows, order = gradient.shape[1:]
    quarter = order // groups
    chunk = order // 4
    struct = jax.ShapeDtypeStruct
    swap = [(0, 1), (1, 0)]

    stats = packed(stats_partial.reshape(2 * blocks, local_rows, order))
    out_shape = (2 * groups, each // 2, 24, chunk)
    outgoing, order_info, place = call(
        functools.partial(pack_stats_body, groups=groups, columns=columns),
        (struct(out_shape, bf16), struct((1, blocks), i32), struct((1, 128), i32)),
        [ANY, ANY, ANY],
        [
            pltpu.VMEM((1, blocks), i32),
            pltpu.SMEM((LAYERS,), i32),
            pltpu.VMEM(stats.shape, f32),
            pltpu.VMEM(out_shape, bf16),
            pltpu.SMEM((1, blocks), i32),
            pltpu.SemaphoreType.DMA((4 + groups,)),
        ],
        (ANY, VMEM, VMEM),
    )(in_hbm(owner_of[None]), in_hbm(layer_count), in_hbm(stats))
    order_info, place = held(order_info), held(place)
    arrived = lax.all_to_all(outgoing, ("dp", "c"), 0, 0, tiled=True)
    grad = packed(gradient)
    grad_half = call(
        functools.partial(grad_half_body, groups=groups, blocks=blocks),
        pltpu.VMEM((each, 8, chunk), bf16),
        [SMEM, VMEM],
    )(order_info, grad)
    grad_theirs = lax.ppermute(grad_half, "c", swap)
    summed = call(
        functools.partial(sum_stats_body, groups=groups, blocks=blocks),
        pltpu.VMEM((columns, 40, chunk), bf16),
        [VMEM, VMEM, VMEM, VMEM],
        [pltpu.SMEM((1, blocks), i32), pltpu.SemaphoreType.DMA],
    )(order_info, held(arrived), grad, held(grad_theirs))
    statistic = lax.all_to_all(summed, ("z", "y"), 0, 0, tiled=True)
    bundle_shape = (order + order // 2, order)
    bundle = call(
        newton_body, pltpu.VMEM(bundle_shape, bf16), [VMEM], [pltpu.VMEM((order, order), f32)]
    )(held(statistic))
    other = lax.ppermute(bundle, "c", swap)
    *quarters, norms = call(
        raw_body,
        tuple(pltpu.VMEM((quarter, order), bf16) for _ in range(groups))
        + (pltpu.VMEM((groups * columns, 1, LANES), f32),),
        [VMEM, VMEM, VMEM],
        [pltpu.VMEM((order, order), bf16), pltpu.SMEM(place.shape, i32), pltpu.SemaphoreType.DMA],
        (VMEM,) * (groups + 1),
    )(place, held(bundle), held(other))
    norms = lax.all_to_all(norms, ("dp", "z", "y"), 0, 0, tiled=True)
    spread = [held(quarters[0])]
    for step in range(1, groups):
        pairs = [(i, (i + step) % groups) for i in range(groups)]
        spread.append(held(lax.ppermute(quarters[step], "dp", pairs)))
    out_shape = (OCAP, quarter, order)
    out = call(
        scale_body,
        struct(out_shape, bf16),
        [VMEM] * (groups + 2),
        [
            pltpu.VMEM(out_shape, bf16),
            pltpu.SMEM(place.shape, i32),
            pltpu.SemaphoreType.DMA((1 + OCAP,)),
        ],
        ANY,
    )(place, held(norms), *spread)
    return out[None]


def solution(mesh):
    shards = mesh.shape["shard"]
    side = 1
    while (2 * side) ** 2 * 2 <= shards:
        side *= 2
    torus = Mesh(
        mesh.devices.reshape(mesh.shape["dp"], shards // (2 * side), side, 2), ("dp", "z", "y", "c")
    )
    placed = (P("dp", None, None, SHARD, None), P(None, SHARD, None), P(), P())
    return jax.shard_map(
        on_device,
        mesh=torus,
        in_specs=placed,
        out_specs=P(SHARD, None, "dp", None),
        check_vma=False,
    )
```

```python
import functools

import jax
import jax.numpy as jnp
from jax import lax
from jax.experimental import pallas as pl
from jax.experimental.pallas import tpu as pltpu
from jax.sharding import Mesh
from jax.sharding import PartitionSpec as P

OCAP = 2
LAYERS = 4
LANES = 128
SHARD = ("z", "y", "c")
bf16, f32, i32 = jnp.bfloat16, jnp.float32, jnp.int32
SMEM = pl.BlockSpec(memory_space=pltpu.SMEM)
VMEM = pl.BlockSpec(memory_space=pltpu.VMEM)


ANY = pl.BlockSpec(memory_space=pl.ANY)


def bits(size):
    assert size & (size - 1) == 0
    return size.bit_length() - 1


def held(x):
    return pltpu.with_memory_space_constraint(x, pltpu.VMEM)


def in_hbm(x):
    return pltpu.with_memory_space_constraint(x, pltpu.HBM)


def call(body, out_shape, in_specs, scratch=(), out_specs=None):
    return pl.pallas_call(
        body,
        out_shape=out_shape,
        in_specs=in_specs,
        out_specs=VMEM if out_specs is None else out_specs,
        scratch_shapes=list(scratch),
        compiler_params=pltpu.CompilerParams(vmem_limit_bytes=24 * 2**20),
    )


def square_sum(x):
    rows, width = x.shape
    return jnp.sum(jnp.sum((x * x).reshape(rows // 8, 8, width), axis=0), keepdims=True)


def packed(x):
    n, r, width = x.shape
    return x.reshape(n, r, 4, width // 4).transpose(0, 2, 1, 3).reshape(n, 4 * r, width // 4)


SINGLE = (3, 2, 0, 1)
MISSING = (2, 3, 1, 0)


def joined(first, second):
    top = lax.broadcasted_iota(i32, first.shape, 0) < 4
    even = jnp.where(top, first, pltpu.roll(second, 4, 0))
    odd = jnp.where(top, pltpu.roll(first, 4, 0), second)
    return even, odd


def index_body(owner_ref, count_ref, sorted_ref, place_ref, *, groups, columns):
    blocks = owner_ref.shape[1]
    me_x, me_c, me_column = lax.axis_index("dp"), lax.axis_index("c"), lax.axis_index(("z", "y"))
    owner = owner_ref[...]
    row = jnp.broadcast_to(owner, (blocks, blocks))
    col = row.T
    sub = lax.broadcasted_iota(i32, row.shape, 0)
    lane = lax.broadcasted_iota(i32, row.shape, 1)
    same = (col == row) & (sub < lane)
    rank = jnp.sum(jnp.where((col < row) | same, 1, 0), axis=0, keepdims=True)
    slot = jnp.sum(jnp.where(same, 1, 0), axis=0, keepdims=True)
    one_lane = lax.broadcasted_iota(i32, owner.shape, 1)
    layer = jnp.zeros(owner.shape, i32)
    end = jnp.int32(0)
    for number in range(LAYERS - 1):
        end = end + count_ref[number]
        layer = layer + jnp.where(one_lane >= end, 1, 0)
    owner_at = bits(blocks)
    layer_at = owner_at + bits(2 * columns)
    slot_at = layer_at + bits(LAYERS)
    top = slot_at + bits(OCAP)
    info = one_lane + (owner << owner_at) + (layer << layer_at) + (slot << slot_at)
    both = jnp.broadcast_to(info + (rank << top), row.shape).T
    ordered = jnp.sum(
        jnp.where((both >> top) == lane, both & ((1 << top) - 1), 0), axis=0, keepdims=True
    )
    sorted_ref[...] = ordered
    ordered_owner = (ordered >> owner_at) & (2 * columns - 1)
    group = one_lane & (groups - 1)
    coded = ordered + ((group + 1) << top)

    def lookup(mask):
        found = jnp.sum(jnp.where(mask, coded, 0), axis=1, keepdims=True)
        live = jnp.where(found > 0, 1, 0)
        source = jnp.maximum((found >> top) - 1, 0)
        return live, source, (found >> layer_at) & (LAYERS - 1), (found >> owner_at) & 1

    live, _, my_layer, core = lookup(((ordered_owner >> 1) == me_column) & (group == me_x))
    place = [live, core, my_layer]
    for s in range(OCAP):
        mask = (ordered_owner == me_column * 2 + me_c) & ((ordered >> slot_at) == s)
        place += list(lookup(mask)[:3])
    wide = lax.broadcasted_iota(i32, place_ref.shape, 1)
    out = jnp.zeros(place_ref.shape, i32)
    for number, value in enumerate(place):
        out = jnp.where(wide == number, value, out)
    place_ref[...] = out


def pack_stats_body(
    owner_ref,
    count_ref,
    stats_ref,
    out_ref,
    sorted_ref,
    place_ref,
    owner_vmem,
    count_smem,
    stats_vmem,
    out_vmem,
    order_ref,
    sems,
    *,
    groups,
    columns,
):
    blocks = owner_ref.shape[1]
    pairs_each = out_ref.shape[1]
    small = [
        pltpu.make_async_copy(owner_ref, owner_vmem, sems.at[1]),
        pltpu.make_async_copy(count_ref, count_smem, sems.at[2]),
    ]
    load = pltpu.make_async_copy(stats_ref, stats_vmem, sems.at[0])
    for copy in small:
        copy.start()
    load.start()
    for copy in small:
        copy.wait()
    index_body(owner_vmem, count_smem, sorted_ref, place_ref, groups=groups, columns=columns)
    move = pltpu.make_async_copy(sorted_ref, order_ref, sems.at[3])
    move.start()
    move.wait()
    load.wait()
    stores = []
    row_block = lax.axis_index(("z", "y")) * 8 // out_ref.shape[3]
    paired = pl.ds(pl.multiple_of(8 * (row_block >> 1), 8), 8)
    single = pl.ds(pl.multiple_of(8 * (1 - (row_block >> 1)), 8), 8)
    lower = ((row_block + 1) & 2) == 0
    for x in range(groups):

        def step(i, carry, x=x):
            places = []
            for k in range(2):
                info = order_ref[0, (2 * i + k) * groups + x]
                places.append((2 * (info & (blocks - 1)), (info >> bits(blocks)) & 1))
            for c in range(2):
                slabs = [block + (core ^ c) for block, core in places]
                pairs = [stats_vmem[slab, paired, :] for slab in slabs]
                even, odd = joined(*[stats_vmem[slab, single, :] for slab in slabs])
                out_vmem[x * 2 + c, i, 0:16] = jnp.concatenate(pairs, axis=0).astype(bf16)
                out_vmem[x * 2 + c, i, 16:24] = jnp.where(lower, odd, even).astype(bf16)
            return carry

        lax.fori_loop(0, pairs_each, step, 0, unroll=4 if pairs_each % 4 == 0 else 1)
        part = pl.ds(2 * x, 2)
        stores.append(pltpu.make_async_copy(out_vmem.at[part], out_ref.at[part], sems.at[4 + x]))
        stores[-1].start()
    for store in stores:
        store.wait()


def grad_half_body(order_ref, grad_ref, out_ref, *, groups, blocks):
    me = lax.axis_index("dp")
    at = 8 * (1 - lax.axis_index("c"))

    def step(k, carry):
        block = order_ref[0, k * groups + me] & (blocks - 1)
        out_ref[k] = grad_ref[block, pl.ds(pl.multiple_of(at, 8), 8), :]
        return carry

    each = blocks // groups
    lax.fori_loop(0, each, step, 0, unroll=8 if each % 8 == 0 else 1)


def sum_stats_body(info_ref, got_ref, grad_ref, theirs_ref, out_ref, order_ref, sem, *, groups, blocks, tall, wide):
    move = pltpu.make_async_copy(info_ref, order_ref, sem)
    move.start()
    out_ref[...] = jnp.zeros(out_ref.shape, bf16)
    move.wait()
    me = lax.axis_index("dp")
    core = lax.axis_index("c")
    half = pl.ds(pl.multiple_of(8 * core, 8), 8)

    def step(i, carry):
        sums = []
        for c in range(2):
            total = got_ref[c, i].astype(f32)
            for x in range(1, groups):
                total = total + got_ref[2 * x + c, i].astype(f32)
            sums.append(total)
        joints = [joined(sums[0][8 * v : 8 * v + 8], sums[1][8 * v : 8 * v + 8]) for v in range(3)]
        for k in range(2):
            info = order_ref[0, (2 * i + k) * groups + me]
            column = (info >> (bits(blocks) + 1)) & (out_ref.shape[0] - 1)
            column = ((column & (wide - 1)) << bits(tall)) + (column >> bits(wide))
            mine = grad_ref[info & (blocks - 1), half, :].astype(f32)
            theirs = theirs_ref[2 * i + k].astype(f32)
            grad = joined(jnp.where(core == 0, mine, theirs), jnp.where(core == 0, theirs, mine))
            out_ref[column, 0:16] = jnp.concatenate(joints[k], axis=0).astype(bf16)
            rest = jnp.concatenate([joints[2][k], grad[0]], axis=0)
            out_ref[column, 16:32] = rest.astype(bf16)
            out_ref[column, 32:40] = grad[1].astype(bf16)
        return carry

    pairs = got_ref.shape[1]
    lax.fori_loop(0, pairs, step, 0, unroll=2 if pairs % 2 == 0 else 1)


def dot(a, b):
    return jnp.dot(a, b, preferred_element_type=f32)


def newton_body(got_ref, out_ref, a_ref, *, tall, wide):
    order = out_ref.shape[1]
    chunk = got_ref.shape[2]

    def column(number):
        tiles = [
            got_ref[pl.ds(z, wide, stride=tall), 8 * number : 8 * number + 8, :].astype(f32)
            for z in range(tall)
        ]
        return jnp.concatenate([tile.reshape(8 * wide, chunk) for tile in tiles], axis=0)

    for number in range(3):
        tiles = column(number)
        for row in range(4):
            q = (row // 2 * 2, row // 2 * 2 + 1, SINGLE[row])[number]
            rows = slice(row * chunk, (row + 1) * chunk)
            a_ref[rows, q * chunk : (q + 1) * chunk] = tiles[rows]
            if MISSING[q] == row:
                a_ref[q * chunk : (q + 1) * chunk, rows] = tiles[rows].T
    for q in range(2):
        tile = column(3 + q).astype(bf16)
        for v in range(2):
            place = slice((2 * v + q) * chunk, (2 * v + q + 1) * chunk)
            out_ref[order:, place] = tile[v * order // 2 : (v + 1) * order // 2]
    a = a_ref[...]
    mean = square_sum(a) * (1.0 / (order * order))
    magnitude = order * jnp.sqrt(mean + 1e-06)
    n = a * (0.25 / magnitude)
    nb = n.astype(bf16)
    e = dot(nb, nb) - 2.5 * n
    eb = e.astype(bf16)
    h = dot(eb, eb) + 3.125 * e
    n1 = dot(h.astype(bf16), nb) + 2.44140625 * n
    n1b = n1.astype(bf16)
    d = dot(nb, n1b) - 1.25 * (n + n1)
    e1 = dot(n1b, n1b) - 2.5 * n1
    e1b = e1.astype(bf16)
    h1 = dot(e1b, e1b) + 3.125 * e1
    n2 = dot(h1.astype(bf16), n1b) + 2.44140625 * n1
    x = 1.25 * d - 1.5625 * n2 - dot(d.astype(bf16), n2.astype(bf16))
    diagonal = lax.broadcasted_iota(i32, x.shape, 0) == lax.broadcasted_iota(i32, x.shape, 1)
    x = x + jnp.where(diagonal, 1.953125, 0.0)
    out_ref[0:order] = (x * (1.0 / jnp.sqrt(jnp.sqrt(magnitude)))).astype(bf16)


def raw_body(scalars_ref, mine_ref, other_ref, *refs):
    norm_ref, raw_ref, place_ref, sem = refs[-4:]
    out_refs = refs[:-4]
    move = pltpu.make_async_copy(scalars_ref, place_ref, sem)
    move.start()
    groups = len(out_refs)
    order = mine_ref.shape[1]
    half, quarter = order // 2, order // groups
    me_c, me_x = lax.axis_index("c"), lax.axis_index("dp")
    grad_sq = square_sum(mine_ref[order:].astype(f32)) + square_sum(other_ref[order:].astype(f32))
    move.wait()
    live, core, layer = place_ref[0, 0], place_ref[0, 1], place_ref[0, 2]
    lane = lax.broadcasted_iota(i32, (1, LANES), 1)

    def finish(left_ref, right_ref):
        raw = jnp.zeros((order, order), f32)
        for ref, at in ((mine_ref, me_c), (other_ref, 1 - me_c)):
            middle = jnp.zeros((order, half), f32)
            for v in range(2):
                cols = slice(v * half, (v + 1) * half)
                middle = middle + dot(left_ref[0:order, cols], ref[order:, cols])
            right = right_ref[pl.ds(pl.multiple_of(at * half, half), half), :]
            raw = raw + dot(middle.astype(bf16), right)
        raw_sq = square_sum(raw)
        norms = jnp.where(lane == layer, grad_sq, 0.0)
        norms = norms + jnp.where(lane == layer + LAYERS, raw_sq, 0.0)
        norms = jnp.where(live > 0, norms, 0.0)
        norm_ref[...] = jnp.broadcast_to(norms[:, None, :], norm_ref.shape)
        raw_ref[...] = raw.astype(bf16)

    @pl.when(core == me_c)
    def _():
        finish(mine_ref, other_ref)

    @pl.when(core != me_c)
    def _():
        finish(other_ref, mine_ref)

    for number, out_ref in enumerate(out_refs):
        start = ((me_x + number) & (groups - 1)) * quarter
        out_ref[...] = raw_ref[pl.ds(pl.multiple_of(start, quarter), quarter), :]


def scale_body(scalars_ref, norm_ref, raw_ref, *refs):
    out_ref, out_vmem, place_ref, sems = refs[-4:]
    others = refs[:-4]
    groups = len(others) + 1
    move = pltpu.make_async_copy(scalars_ref, place_ref, sems.at[0])
    move.start()
    chains = 8
    length = norm_ref.shape[0] // chains
    total = jnp.zeros((1, LANES), f32)
    for number in range(chains):
        total = total + jnp.sum(norm_ref[number * length : (number + 1) * length], axis=0)
    lane = lax.broadcasted_iota(i32, (1, LANES), 1)
    me_x = lax.axis_index("dp")
    move.wait()
    stores = []
    for s in range(OCAP):
        live, source, layer = place_ref[0, 3 + 3 * s], place_ref[0, 4 + 3 * s], place_ref[0, 5 + 3 * s]
        grad_total = jnp.sum(jnp.where(lane == layer, total, 0.0), keepdims=True)
        raw_total = jnp.sum(jnp.where(lane == layer + LAYERS, total, 0.0), keepdims=True)
        ratio = jnp.sqrt((grad_total + 1e-06) / (raw_total + 1e-06))
        step = jnp.where(live > 0, (me_x - source) & (groups - 1), groups)
        for number in range(groups):

            @pl.when(step == number)
            def _(number=number, s=s, ratio=ratio):
                block = raw_ref[...] if number == 0 else others[number - 1][...]
                out_vmem[s] = (block.astype(f32) * ratio).astype(bf16)

        @pl.when(step == groups)
        def _(s=s):
            out_vmem[s] = jnp.zeros(out_vmem.shape[1:], bf16)

        stores.append(pltpu.make_async_copy(out_vmem.at[s], out_ref.at[s], sems.at[1 + s]))
        stores[-1].start()
    for store in stores:
        store.wait()


def on_device(stats_partial, gradient, owner_of, layer_count):
    groups = lax.axis_size("dp")
    columns = lax.axis_size("z") * lax.axis_size("y")
    blocks = owner_of.shape[0]
    each = blocks // groups
    local_rows, order = gradient.shape[1:]
    quarter = order // groups
    chunk = order // 4
    struct = jax.ShapeDtypeStruct
    swap = [(0, 1), (1, 0)]
    sides = dict(tall=lax.axis_size("z"), wide=lax.axis_size("y"))

    stats = packed(stats_partial.reshape(2 * blocks, local_rows, order))
    out_shape = (2 * groups, each // 2, 24, chunk)
    outgoing, order_info, place = call(
        functools.partial(pack_stats_body, groups=groups, columns=columns),
        (struct(out_shape, bf16), struct((1, blocks), i32), struct((1, 128), i32)),
        [ANY, ANY, ANY],
        [
            pltpu.VMEM((1, blocks), i32),
            pltpu.SMEM((LAYERS,), i32),
            pltpu.VMEM(stats.shape, f32),
            pltpu.VMEM(out_shape, bf16),
            pltpu.SMEM((1, blocks), i32),
            pltpu.SemaphoreType.DMA((4 + groups,)),
        ],
        (ANY, VMEM, VMEM),
    )(in_hbm(owner_of[None]), in_hbm(layer_count), in_hbm(stats))
    order_info, place = held(order_info), held(place)
    arrived = lax.all_to_all(outgoing, ("dp", "c"), 0, 0, tiled=True)
    grad = packed(gradient)
    grad_half = call(
        functools.partial(grad_half_body, groups=groups, blocks=blocks),
        pltpu.VMEM((each, 8, chunk), bf16),
        [SMEM, VMEM],
    )(order_info, grad)
    grad_theirs = lax.ppermute(grad_half, "c", swap)
    summed = call(
        functools.partial(sum_stats_body, groups=groups, blocks=blocks, **sides),
        pltpu.VMEM((columns, 40, chunk), bf16),
        [VMEM, VMEM, VMEM, VMEM],
        [pltpu.SMEM((1, blocks), i32), pltpu.SemaphoreType.DMA],
    )(order_info, held(arrived), grad, held(grad_theirs))
    statistic = lax.all_to_all(summed, ("y", "z"), 0, 0, tiled=True)
    bundle_shape = (order + order // 2, order)
    bundle = call(
        functools.partial(newton_body, **sides),
        pltpu.VMEM(bundle_shape, bf16),
        [VMEM],
        [pltpu.VMEM((order, order), f32)],
    )(held(statistic))
    other = lax.ppermute(bundle, "c", swap)
    *quarters, norms = call(
        raw_body,
        tuple(pltpu.VMEM((quarter, order), bf16) for _ in range(groups))
        + (pltpu.VMEM((groups * columns, 1, LANES), f32),),
        [VMEM, VMEM, VMEM],
        [pltpu.VMEM((order, order), bf16), pltpu.SMEM(place.shape, i32), pltpu.SemaphoreType.DMA],
        (VMEM,) * (groups + 1),
    )(place, held(bundle), held(other))
    norms = lax.all_to_all(norms, ("y", "z", "dp"), 0, 0, tiled=True)
    spread = [held(quarters[0])]
    for step in range(1, groups):
        pairs = [(i, (i + step) % groups) for i in range(groups)]
        spread.append(held(lax.ppermute(quarters[step], "dp", pairs)))
    out_shape = (OCAP, quarter, order)
    out = call(
        scale_body,
        struct(out_shape, bf16),
        [VMEM] * (groups + 2),
        [
            pltpu.VMEM(out_shape, bf16),
            pltpu.SMEM(place.shape, i32),
            pltpu.SemaphoreType.DMA((1 + OCAP,)),
        ],
        ANY,
    )(place, held(norms), *spread)
    return out[None]


def solution(mesh):
    shards = mesh.shape["shard"]
    side = 1
    while (2 * side) ** 2 * 2 <= shards:
        side *= 2
    torus = Mesh(
        mesh.devices.reshape(mesh.shape["dp"], shards // (2 * side), side, 2), ("dp", "z", "y", "c")
    )
    placed = (P("dp", None, None, SHARD, None), P(None, SHARD, None), P(), P())
    return jax.shard_map(
        on_device,
        mesh=torus,
        in_specs=placed,
        out_specs=P(SHARD, None, "dp", None),
        check_vma=False,
    )
```
